512 devices in a mesh: section: 4 (over x), dom: 128 (over z, y, core).
Axes of the slice: x: 4, y: 8, z: 8, core: 2. Of those that a mesh axis runs over, the one named last changes fastest.
Arguments:
- features: bfloat16 [2, 32768, 128], P(None, 'dom'), may hold values from -6 to 6
- input_weight: bfloat16 [128, 512], replicated, may hold values from -0.5 to 0.5
- layer_weights: bfloat16 [8, 512, 512], P('section'), may hold values from -0.25 to 0.25
- tiles: bfloat16 [2, 256, 4, 128, 128], P(None, 'dom'), may hold values from -0.4375 to 0.4375
- pub_ids: int32 [2, 256], P(None, 'dom'), may hold values from -1 to 1, as said below
- tile_src: int32 [2, 256, 4], P(None, 'dom'), may hold values from 0 to 5, as said below
Outputs:
- section_outputs: bfloat16 [4, 2, 32768, 512], P('section', None, 'dom')
The draws below stay inside these ranges and needn't reach their ends.
Inputs may be any that keep to these rules, and one draw needn't show every extreme that they name: `pub_ids`: for each node group and partition, its 2 slots hold distinct local block numbers below 2 first and -1 in the unused slots after them; every partition lists at least one block, and in every node group some partition fills all 2 slots. `tile_src`: each entry names a slot of the destination block's partition: a local block below 2, or a listed (not -1) slot of the previous or the next partition; the first partition reads no previous one and the last no next one. In every node group some tile reads the last slot of a next partition.
All inputs are finite; a program needn't handle non-finite values.
Results may differ from the reference program's by a relative error of at most 0.019.
Values may be sent and summed in bfloat16 or wider, within the bound.
A program may use at most 64 MiB of HBM per device.

```python
import jax
import jax.numpy as jnp
from jax import lax

D = 512
D_IN = 128
BS = 128
NB = 2
K = 4
BMAX = 2
GROUPS = 2
LPS = 2
LAYERS = 8
NBLK = 256
NODES = 32768
N_SECTION = 4
N_DOM = 128


def boundary_plan(key):
    count_key = jax.random.fold_in(key, 101)
    force_key = jax.random.fold_in(key, 102)
    order_key = jax.random.fold_in(key, 103)
    counts = jax.random.randint(count_key, (GROUPS, N_DOM), 1, BMAX + 1)
    forced = jax.random.randint(force_key, (GROUPS,), 1, N_DOM)
    counts = counts.at[jnp.arange(GROUPS), forced].set(BMAX)
    order_keys = jax.random.split(order_key, GROUPS * N_DOM)
    orders = jax.vmap(lambda single: jax.random.permutation(single, NB))(order_keys)
    orders = orders.reshape(GROUPS, N_DOM, NB)[:, :, :BMAX]
    listed = jnp.where(jnp.arange(BMAX)[None, None, :] < counts[:, :, None], orders, -1)
    return (counts.astype(jnp.int32), listed.astype(jnp.int32), forced.astype(jnp.int32))


def draw_pub_ids(key, part):
    counts, listed, forced = boundary_plan(key)
    return listed.reshape(GROUPS, N_DOM * BMAX)


def draw_tile_src(key, part):
    counts, listed, forced = boundary_plan(key)
    block_ids = jnp.arange(N_DOM * NB)
    device = block_ids // NB
    own_block = block_ids % NB
    grid_shape = (GROUPS, N_DOM * NB)
    left_count = counts[:, jnp.clip(device - 1, 0, N_DOM - 1)]
    right_count = counts[:, jnp.clip(device + 1, 0, N_DOM - 1)]
    columns = [jnp.broadcast_to(own_block, grid_shape)]
    columns.append(jax.random.randint(jax.random.fold_in(key, 201), grid_shape, 0, NB))
    left_pick = NB + jax.random.randint(jax.random.fold_in(key, 202), grid_shape, 0, left_count)
    left_other = jax.random.randint(jax.random.fold_in(key, 203), grid_shape, 0, NB)
    columns.append(jnp.where(device[None, :] > 0, left_pick, left_other))
    right_pick = NB + BMAX + jax.random.randint(jax.random.fold_in(key, 204), grid_shape, 0, right_count)
    reach_block = (forced - 1) * NB
    right_pick = jnp.where(block_ids[None, :] == reach_block[:, None], NB + 2 * BMAX - 1, right_pick)
    right_other = jax.random.randint(jax.random.fold_in(key, 205), grid_shape, 0, NB)
    columns.append(jnp.where(device[None, :] < N_DOM - 1, right_pick, right_other))
    for column_index in range(K - 4):
        columns.append(jax.random.randint(jax.random.fold_in(key, 300 + column_index), grid_shape, 0, NB))
    return jnp.stack(columns, -1).astype(jnp.int32)


def shard_levels(key, extent, cuts, smallest, largest):
    def one(axis_at, parts):
        steps = jax.random.uniform(jax.random.fold_in(jax.random.fold_in(key, 6), axis_at), (parts,), jnp.float32, smallest / len(cuts), largest / len(cuts))
        return jnp.repeat(jnp.exp(steps), extent[axis_at] // parts).reshape((-1,) + (1,) * (len(extent) - axis_at - 1))

    loudness = one(*cuts[0])
    for cut in cuts[1:]:
        loudness = loudness * one(*cut)
    return loudness


def centred(stream_key, dims, scale, most, cuts=(), kind=jnp.bfloat16):
    factor_of = shard_levels(stream_key, dims, cuts, -0.22, 0.18) if cuts else 1.0
    result = jax.random.normal(stream_key, dims, jnp.float32) * scale * factor_of
    return jnp.minimum(jnp.maximum(result, -most), most).astype(kind)


def setup_inputs(seed: int = 0) -> dict:
    streams_of = jax.random.split(jax.random.key(seed), 7)
    return {
        "features": centred(streams_of[0], (GROUPS, NODES, D_IN), 1.0, 6.0, ((1, 128),)),
        "input_weight": centred(streams_of[1], (D_IN, D), D_IN ** -0.5, 0.5),
        "layer_weights": centred(streams_of[2], (LAYERS, D, D), D ** -0.5, 0.25, ((0, 4),)),
        "tiles": centred(streams_of[3], (GROUPS, NBLK, K, BS, BS), (1.7 * (K * BS) ** -0.5), 0.4375, ((1, 128),)),
        "pub_ids": draw_pub_ids(jax.random.fold_in(streams_of[6], 71), 0),
        "tile_src": draw_tile_src(jax.random.fold_in(streams_of[6], 71), 0),
    }


residual_share = 0.1
decay_theta = 0.5


def global_sources(source_slots, listed):
    block_total = source_slots.shape[0]
    device = jnp.arange(block_total, dtype=jnp.int32) // NB
    left_dev = jnp.clip(device - 1, 0, N_DOM - 1)
    right_dev = jnp.clip(device + 1, 0, N_DOM - 1)
    middle = jnp.clip(source_slots - NB, 0, BMAX - 1)
    farther = jnp.clip(source_slots - NB - BMAX, 0, BMAX - 1)
    from_left = listed[left_dev[:, None], middle]
    from_right = listed[right_dev[:, None], farther]
    global_ids = jnp.where(source_slots < NB, device[:, None] * NB + source_slots,
                           jnp.where(source_slots < NB + BMAX, left_dev[:, None] * NB + from_left,
                                     right_dev[:, None] * NB + from_right))
    return global_ids.astype(jnp.int32)


def propagate(hidden, initial, group_tiles, global_ids, weight, beta):
    blocks = hidden.reshape(-1, BS, D)

    def per_partition(pair):
        tile_part, id_part = pair
        gathered = jnp.take(blocks, id_part.reshape(-1), axis=0).reshape(NB, K, BS, D)
        return jnp.einsum('bkij,bkjd->bid', tile_part.astype(jnp.float32), gathered.astype(jnp.float32))

    aggregate = lax.map(per_partition, (group_tiles.reshape(N_DOM, NB, K, BS, BS),
                                        global_ids.reshape(N_DOM, NB, K))).reshape(-1, D)
    support = ((1.0 - residual_share) * aggregate + residual_share * initial.astype(jnp.float32)).astype(jnp.bfloat16)
    product = jnp.dot(support, weight, preferred_element_type=jnp.float32)
    mixed = (1.0 - beta) * support.astype(jnp.float32) + beta * product
    return jax.nn.relu(mixed).astype(jnp.bfloat16)


def reference(features, input_weight, layer_weights, tiles, pub_ids, tile_src):
    listed_all = pub_ids.reshape(GROUPS, N_DOM, BMAX)
    results = []
    for group in range(GROUPS):
        initial = jax.nn.relu(jnp.dot(features[group], input_weight, preferred_element_type=jnp.float32)).astype(jnp.bfloat16)
        hidden = initial
        global_ids = global_sources(tile_src[group], listed_all[group])
        per_section = []
        for section_number in range(N_SECTION):
            for inner in range(LPS):
                layer = section_number * LPS + inner
                beta = jnp.log(decay_theta / jnp.float32(layer + 1) + 1.0)
                hidden = propagate(hidden, initial, tiles[group], global_ids, layer_weights[layer], beta)
            per_section.append(hidden)
        results.append(jnp.stack(per_section))
    return jnp.stack(results, axis=1)
```

```python
import functools
import math

import jax
import jax.numpy as jnp
from jax import lax
from jax.experimental import pallas as pl
from jax.experimental.pallas import tpu as pltpu
from jax.sharding import PartitionSpec as P

MESH = pl.DeviceIdType.MESH
SHARE = 0.1
THETA = 0.5


def remote(src, dst, sent, landed, device):
    return pltpu.make_async_remote_copy(
        src_ref=src, dst_ref=dst, send_sem=sent, recv_sem=landed, device_id=device, device_id_type=MESH
    )


def kernel(
    sections, partitions, features, input_weight, weights, tiles, pub_ids, tile_src, out,
    table, last, slab, rows_in, proj, tile_buf, near_op, ghost_op, ints, support,
    local_sem, in_sent, feat_land, int_land, tile_land, near_sent, near_land, far_sent, far_land,
    slab_sent, slab_land, slab_pass, slab_swap, out_sent, out_land,
):
    block_total, tile_total = tiles.shape[1], tiles.shape[2]
    side = tiles.shape[3]
    rows = block_total * side
    half = weights.shape[1] // 2
    per_section = weights.shape[0]
    layers = sections * per_section
    final_section = sections - 1

    section = lax.axis_index("section")
    here = lax.axis_index("dom")
    core = lax.rem(here, 2)
    outward = 2 * core - 1
    wrap = lambda q: lax.rem(q + 2 * partitions, partitions)
    mate = wrap(here + outward)
    partner = wrap(here - outward)
    source = wrap(here + 2 * outward)
    target = wrap(here - 2 * outward)
    chain = (section == 0) | (section == final_section)
    group = jnp.where(section == 0, 1, 0)
    other_group = 1 - group
    at = lambda slot: pl.ds(slot * rows, rows)

    def local_half(layer, which):
        return (
            weights.at[layer - section * per_section, pl.ds(which * half, half)],
            slab.at[layer, pl.ds(which * half, half)],
        )

    feature_load = pltpu.make_async_copy(features.at[group], rows_in.at[at(2)], local_sem.at[0])
    tile_load = pltpu.make_async_copy(tiles.at[group], tile_buf.at[1], local_sem.at[1])
    proj_load = pltpu.make_async_copy(input_weight, proj, local_sem.at[2])

    @pl.when(chain)
    def _():
        feature_load.start()
        proj_load.start()
        tile_load.start()
        for i in range(per_section):
            layer = section * per_section + i
            src, dst = local_half(layer, core)
            pltpu.make_async_copy(src, dst, slab_land.at[layer]).start()
            src, dst = local_half(layer, 1 - core)
            pltpu.make_async_copy(src, dst, slab_swap.at[layer]).start()
        row = lax.broadcasted_iota(jnp.int32, (16, 128), 0)
        packed = jnp.zeros((16, 128), jnp.int32)
        for m in range(2):
            packed = jnp.where(row == m, pub_ids[group, m], packed)
        for b in range(block_total):
            for k in range(tile_total):
                packed = jnp.where(row == 2 + b * tile_total + k, tile_src[group, b, k], packed)
        ints[2] = packed

    barrier = pltpu.get_barrier_semaphore()
    peers = [(section, q) for q in (mate, partner, source, target)]
    peers += [(lax.rem(section + k, sections), here) for k in range(1, sections)]
    for peer in peers:
        pl.semaphore_signal(barrier, inc=1, device_id=peer, device_id_type=MESH)
    pl.semaphore_wait(barrier, len(peers))

    def slab_copy(i, which, plane):
        src = weights.at[i, pl.ds(core * half, half)]
        dst = slab.at[section * per_section + i, pl.ds(core * half, half)]
        landed = slab_land.at[section * per_section + i]
        return remote(src, dst, slab_sent.at[i, which], landed, (plane, here))

    def slab_sends(act):
        for i in range(per_section):
            for which, plane in enumerate((0, final_section)):
                @pl.when(section != plane)
                def _():
                    act(slab_copy(i, which, plane))

    def slab_forward(layer):
        part = slab.at[layer, pl.ds(core * half, half)]
        return remote(part, part, slab_pass.at[layer], slab_swap.at[layer], (section, partner))

    def near_copy(layer):
        return remote(
            table.at[layer, at(2)], table.at[layer, at(3)], near_sent.at[layer], near_land.at[layer],
            (section, partner),
        )

    def far_copy(layer):
        return remote(
            table.at[layer, at(2)], table.at[layer, at(0)], far_sent.at[layer], far_land.at[layer],
            (section, target),
        )

    def out_copy(state, plane):
        return remote(
            state, out.at[0, group], out_sent.at[plane], out_land.at[group], (plane, here)
        )

    def out_local(state):
        return pltpu.make_async_copy(state, out.at[0, group], local_sem.at[3])

    int_dests = ((0, target), (1, mate), (3, partner))

    def int_copy(n):
        slot, q = int_dests[n]
        return remote(ints.at[2], ints.at[slot], in_sent.at[n], int_land.at[slot], (section, q))

    def feature_copy(n):
        slot, q = int_dests[n]
        return remote(
            features.at[group], rows_in.at[at(slot)], in_sent.at[3 + n], feat_land.at[slot], (section, q)
        )

    tile_copy = remote(tiles.at[group], tile_buf.at[0], in_sent.at[6], tile_land.at[0], (section, mate))

    @pl.when(chain)
    def _():
        for n in (1, 2, 0):
            feature_copy(n).start()
        for n in range(3):
            int_copy(n).start()
        tile_copy.start()

    slab_sends(lambda copy: copy.start())

    def build(op, tile_slot, int_slot, outer, inner):
        outer_pub = [ints[outer, m : m + 1, :] for m in range(2)]
        inner_pub = [ints[inner, m : m + 1, :] for m in range(2)]
        before = [jnp.where(core == 0, a, 4 + b) for a, b in zip(outer_pub, inner_pub)]
        after = [jnp.where(core == 0, 4 + b, a) for a, b in zip(outer_pub, inner_pub)]
        for b in range(block_total):
            columns = []
            for k in range(tile_total):
                n = 2 + b * tile_total + k
                slot = ints[int_slot, n : n + 1, :]
                column = jnp.where(slot < 2, 2 + slot, after[1])
                column = jnp.where(slot == 2, before[0], column)
                column = jnp.where(slot == 3, before[1], column)
                column = jnp.where(slot == 4, after[0], column)
                columns.append(column)
            pieces = [tile_buf[tile_slot, b, k].astype(jnp.float32) for k in range(tile_total)]
            for j in range(6):
                total = jnp.zeros((side, side), jnp.float32)
                for k in range(tile_total):
                    total += pieces[k] * (columns[k] == j).astype(jnp.float32)
                op[b * side : (b + 1) * side, j * side : (j + 1) * side] = total.astype(jnp.bfloat16)

    def propagate(op, layer, base, dst):
        beta = jnp.float32(0.0)
        for i in range(layers):
            beta = jnp.where(layer == i, jnp.float32(math.log(THETA / (i + 1) + 1.0)), beta)
        aggregate = jnp.dot(
            op[...], table[layer, base * rows : (base + 3) * rows, :], preferred_element_type=jnp.float32
        )
        initial = table[0, (base + 1) * rows : (base + 2) * rows, :].astype(jnp.float32)
        support[...] = ((1.0 - SHARE) * aggregate + SHARE * initial).astype(jnp.bfloat16)
        product = jnp.dot(support[...], slab[layer], preferred_element_type=jnp.float32)
        mixed = (1.0 - beta) * support[...].astype(jnp.float32) + beta * product
        dst[...] = jnp.maximum(mixed, 0.0).astype(jnp.bfloat16)

    def slab_ready(layer):
        slab_forward_half = slab.at[layer, pl.ds(core * half, half)]
        pltpu.make_async_copy(slab_forward_half, slab_forward_half, slab_land.at[layer]).wait()

        @pl.when(layer // per_section != section)
        def _():
            slab_forward(layer).start()

    def slab_swapped(layer):
        part = slab.at[layer, pl.ds((1 - core) * half, half)]
        pltpu.make_async_copy(part, part, slab_swap.at[layer]).wait()

    @pl.when(chain)
    def _():
        feature_load.wait()
        proj_load.wait()
        for n in (2, 1, 0):
            feature_copy(n).wait_recv()
        table[0] = jnp.maximum(
            jnp.dot(rows_in[...], proj[...], preferred_element_type=jnp.float32), 0.0
        ).astype(jnp.bfloat16)
        tile_load.wait()
        for n in range(3):
            int_copy(n).wait_recv()
        build(near_op, 1, 2, 1, 3)
        slab_ready(0)

        def step(layer, carry):
            slab_swapped(layer)

            @pl.when(layer > 0)
            def _():
                near_copy(layer).wait_recv()

            propagate(near_op, layer, 1, table.at[layer + 1, at(2)])
            near_copy(layer + 1).start()

            @pl.when(layer < layers - 2)
            def _():
                far_copy(layer + 1).start()

            @pl.when(lax.rem(layer + 1, per_section) == 0)
            def _():
                plane = (layer + 1) // per_section - 1
                state = table.at[layer + 1, at(2)]

                @pl.when(plane == section)
                def _():
                    out_local(state).start()

                @pl.when(plane != section)
                def _():
                    out_copy(state, plane).start()

            slab_ready(layer + 1)

            @pl.when(layer == 0)
            def _():
                tile_copy.wait_recv()
                build(ghost_op, 0, 1, 0, 2)

            @pl.when(layer > 0)
            def _():
                far_copy(layer).wait_recv()

            propagate(ghost_op, layer, 0, table.at[layer + 1, at(1)])
            return carry

        lax.fori_loop(0, layers - 1, step, 0)
        end = layers - 1
        slab_swapped(end)
        near_copy(end).wait_recv()
        propagate(near_op, end, 1, last)

        @pl.when(section == final_section)
        def _():
            out_local(last).start()

        @pl.when(section != final_section)
        def _():
            out_copy(last, final_section).start()

        for n in range(3):
            int_copy(n).wait_send()
            feature_copy(n).wait_send()
        tile_copy.wait_send()
        for layer in range(1, layers):
            near_copy(layer).wait_send()
            if layer < layers - 1:
                far_copy(layer).wait_send()
        for layer in range(layers):
            @pl.when(layer // per_section != section)
            def _():
                slab_forward(layer).wait_send()
        for plane in range(sections):
            @pl.when(plane != section)
            def _():
                out_copy(last, plane).wait_send()
        out_local(last).wait()

        arriving = out.at[0, other_group]
        pltpu.make_async_copy(arriving, arriving, out_land.at[other_group]).wait()

    @pl.when(jnp.logical_not(chain))
    def _():
        for g in range(2):
            pltpu.make_async_copy(out.at[0, g], out.at[0, g], out_land.at[g]).wait()

    slab_sends(lambda copy: copy.wait_send())


def shards(features, input_weight, layer_weights, tiles, pub_ids, tile_src):
    groups, rows, width_in = features.shape
    width = input_weight.shape[1]
    block_total, tile_total, side = tiles.shape[1:4]
    per_section = layer_weights.shape[0]
    sections = lax.axis_size("section")
    partitions = lax.axis_size("dom")
    layers = sections * per_section
    anywhere = pl.BlockSpec(memory_space=pl.ANY)
    scalars = pl.BlockSpec(memory_space=pltpu.SMEM)
    dma = pltpu.SemaphoreType.DMA
    bf16 = jnp.bfloat16
    return pl.pallas_call(
        functools.partial(kernel, sections, partitions),
        out_shape=jax.ShapeDtypeStruct((1, groups, rows, width), bf16),
        in_specs=[anywhere] * 4 + [scalars] * 2,
        out_specs=anywhere,
        scratch_shapes=[
            pltpu.VMEM((layers, 4 * rows, width), bf16),
            pltpu.VMEM((rows, width), bf16),
            pltpu.VMEM((layers, width, width), bf16),
            pltpu.VMEM((4 * rows, width_in), bf16),
            pltpu.VMEM((width_in, width), bf16),
            pltpu.VMEM((2, block_total, tile_total, side, side), bf16),
            pltpu.VMEM((rows, 3 * rows), bf16),
            pltpu.VMEM((rows, 3 * rows), bf16),
            pltpu.VMEM((4, 16, 128), jnp.int32),
            pltpu.VMEM((rows, width), bf16),
            dma((4,)),
            dma((7,)),
            dma((4,)),
            dma((4,)),
            dma((1,)),
            dma((layers,)),
            dma((layers,)),
            dma((layers,)),
            dma((layers,)),
            dma((per_section, 2)),
            dma((layers,)),
            dma((layers,)),
            dma((layers,)),
            dma((sections,)),
            dma((groups,)),
        ],
        compiler_params=pltpu.CompilerParams(collective_id=0, has_side_effects=True),
    )(features, input_weight, layer_weights, tiles, pub_ids, tile_src)


def solution(mesh):
    in_specs = (
        P(None, "dom", None),
        P(),
        P("section", None, None),
        P(None, "dom", None, None, None),
        P(None, "dom"),
        P(None, "dom", None),
    )
    out_specs = P("section", None, "dom", None)
    return jax.shard_map(shards, mesh=mesh, in_specs=in_specs, out_specs=out_specs, check_vma=False)
```

```python
import functools
import math

import jax
import jax.numpy as jnp
from jax import lax
from jax.experimental import pallas as pl
from jax.experimental.pallas import tpu as pltpu
from jax.sharding import PartitionSpec as P

MESH = pl.DeviceIdType.MESH
SHARE = 0.1
THETA = 0.5


def remote(src, dst, sent, landed, device):
    return pltpu.make_async_remote_copy(
        src_ref=src, dst_ref=dst, send_sem=sent, recv_sem=landed, device_id=device, device_id_type=MESH
    )


def kernel(
    sections, partitions, features, input_weight, weights, tiles, pub_ids, tile_src, out,
    table, last, slab, rows_in, proj, tile_buf, near_op, ghost_op, ints, support, near_sum, ghost_sum,
    local_sem, in_sent, feat_land, int_land, tile_land, near_sent, near_land, far_sent, far_land,
    slab_sent, slab_land, slab_pass, slab_swap, out_sent, out_land,
):
    block_total, tile_total = tiles.shape[1], tiles.shape[2]
    side = tiles.shape[3]
    rows = block_total * side
    half = weights.shape[1] // 2
    per_section = weights.shape[0]
    layers = sections * per_section
    final_section = sections - 1

    section = lax.axis_index("section")
    here = lax.axis_index("dom")
    core = lax.rem(here, 2)
    outward = 2 * core - 1
    wrap = lambda q: lax.rem(q + 2 * partitions, partitions)
    mate = wrap(here + outward)
    partner = wrap(here - outward)
    source = wrap(here + 2 * outward)
    target = wrap(here - 2 * outward)
    chain = (section == 0) | (section == final_section)
    group = jnp.where(section == 0, 1, 0)
    other_group = 1 - group
    inner = (here != 0) & (here != partitions - 1)
    to_target = (target != 0) & (target != partitions - 1)
    piece = rows // 2
    at = lambda slot: pl.ds(slot * rows, rows)

    def local_half(layer, which):
        return (
            weights.at[layer - section * per_section, pl.ds(which * half, half)],
            slab.at[layer, pl.ds(which * half, half)],
        )

    feature_load = pltpu.make_async_copy(features.at[group], rows_in.at[at(2)], local_sem.at[0])
    tile_load = pltpu.make_async_copy(tiles.at[group], tile_buf.at[1], local_sem.at[1])
    proj_load = pltpu.make_async_copy(input_weight, proj, local_sem.at[2])

    @pl.when(chain)
    def _():
        feature_load.start()
        proj_load.start()
        tile_load.start()
        for i in range(per_section):
            layer = section * per_section + i
            src, dst = local_half(layer, core)
            pltpu.make_async_copy(src, dst, slab_land.at[layer]).start()
            src, dst = local_half(layer, 1 - core)
            pltpu.make_async_copy(src, dst, slab_swap.at[layer]).start()
        row = lax.broadcasted_iota(jnp.int32, (16, 128), 0)
        packed = jnp.zeros((16, 128), jnp.int32)
        for m in range(2):
            packed = jnp.where(row == m, pub_ids[group, m], packed)
        for b in range(block_total):
            for k in range(tile_total):
                packed = jnp.where(row == 2 + b * tile_total + k, tile_src[group, b, k], packed)
        ints[2] = packed

    barrier = pltpu.get_barrier_semaphore()
    peers = [(section, q) for q in (mate, partner, source, target)]
    peers += [(lax.rem(section + k, sections), here) for k in range(1, sections)]
    for peer in peers:
        pl.semaphore_signal(barrier, inc=1, device_id=peer, device_id_type=MESH)
    pl.semaphore_wait(barrier, len(peers))

    def slab_copy(n, layer, plane):
        part = pl.ds(core * half, half)
        if layer // per_section == plane_of[n]:
            src = weights.at[layer % per_section, part]
        else:
            src = slab.at[layer, part]
        return remote(src, slab.at[layer, part], slab_sent.at[n % 5], slab_land.at[layer], (plane, here))

    plane_of = [0] * 5 + [1] * 5 + [2] * 5 + [3] * 5
    routes = {
        0: ((0, 3), (1, 3)),
        1: ((2, 0), (2, 2), (3, 0), (3, 3), (5, 0)),
        2: ((4, 0), (5, 1), (2, 3), (4, 3), (5, 3)),
        3: ((6, 0), (7, 0)),
    }

    def slab_sends(plane):
        return [slab_copy(5 * plane + n, layer, to) for n, (layer, to) in enumerate(routes[plane])]

    def slab_forward(layer):
        part = slab.at[layer, pl.ds(core * half, half)]
        return remote(part, part, slab_pass.at[layer], slab_swap.at[layer], (section, partner))

    def near_copy(layer, m=None):
        src, dst = (at(2), at(3)) if m is None else (pl.ds(2 * rows + m * piece, piece), pl.ds(3 * rows + m * piece, piece))
        return remote(
            table.at[layer, src], table.at[layer, dst], near_sent.at[layer], near_land.at[layer],
            (section, partner),
        )

    def far_copy(layer, m=None):
        src, dst = (at(2), at(0)) if m is None else (pl.ds(2 * rows + m * piece, piece), pl.ds(m * piece, piece))
        return remote(
            table.at[layer, src], table.at[layer, dst], far_sent.at[layer], far_land.at[layer],
            (section, target),
        )

    def out_copy(state, plane, m=None):
        part = pl.ds(0, rows) if m is None else pl.ds(m * piece, piece)
        return remote(
            state, out.at[0, group, part], out_sent.at[plane], out_land.at[group], (plane, here)
        )

    def out_local(state, m=None):
        part = pl.ds(0, rows) if m is None else pl.ds(m * piece, piece)
        return pltpu.make_async_copy(state, out.at[0, group, part], local_sem.at[3])

    int_dests = ((0, target), (1, mate), (3, partner))

    def int_copy(n):
        slot, q = int_dests[n]
        return remote(ints.at[2], ints.at[slot], in_sent.at[n], int_land.at[slot], (section, q))

    def feature_copy(n):
        slot, q = int_dests[n]
        return remote(
            features.at[group], rows_in.at[at(slot)], in_sent.at[3 + n], feat_land.at[slot], (section, q)
        )

    tile_copy = remote(tiles.at[group], tile_buf.at[0], in_sent.at[6], tile_land.at[0], (section, mate))

    takes = (inner, inner, None)
    gives = (to_target, inner, None)

    def each(flags, n, act):
        if flags[n] is None:
            act()
        else:
            pl.when(flags[n])(act)

    @pl.when(chain)
    def _():
        for n in (1, 2, 0):
            each(gives, n, lambda: int_copy(n).start())
        for n in (1, 2, 0):
            each(gives, n, lambda: feature_copy(n).start())
        each(gives, 1, lambda: tile_copy.start())

    for plane in (0, 3):
        @pl.when(section == plane)
        def _():
            for copy in slab_sends(plane):
                copy.start()

    def build(op, tile_slot, int_slot, outer, inner):
        outer_pub = [ints[outer, m : m + 1, :] for m in range(2)]
        inner_pub = [ints[inner, m : m + 1, :] for m in range(2)]
        before = [jnp.where(core == 0, a, 4 + b) for a, b in zip(outer_pub, inner_pub)]
        after = [jnp.where(core == 0, 4 + b, a) for a, b in zip(outer_pub, inner_pub)]
        for b in range(block_total):
            columns = []
            for k in range(tile_total):
                n = 2 + b * tile_total + k
                slot = ints[int_slot, n : n + 1, :]
                column = jnp.where(slot < 2, 2 + slot, after[1])
                column = jnp.where(slot == 2, before[0], column)
                column = jnp.where(slot == 3, before[1], column)
                column = jnp.where(slot == 4, after[0], column)
                columns.append(column)
            pieces = [tile_buf[tile_slot, b, k].astype(jnp.float32) for k in range(tile_total)]
            for j in range(6):
                total = jnp.zeros((side, side), jnp.float32)
                for k in range(tile_total):
                    total += pieces[k] * (columns[k] == j).astype(jnp.float32)
                op[b * side : (b + 1) * side, j * side : (j + 1) * side] = total.astype(jnp.bfloat16)

    def gather(op, layer, base, total):
        total[...] = jnp.dot(
            op[:, rows:], table[layer, (base + 1) * rows : (base + 3) * rows, :], preferred_element_type=jnp.float32
        )

    def propagate(op, layer, base, total, dst, done):
        beta = jnp.float32(0.0)
        for i in range(layers):
            beta = jnp.where(layer == i, jnp.float32(math.log(THETA / (i + 1) + 1.0)), beta)
        for m in range(2):
            part = slice(m * piece, (m + 1) * piece)
            aggregate = total[part, :] + jnp.dot(
                op[part, :rows], table[layer, base * rows : (base + 1) * rows, :], preferred_element_type=jnp.float32
            )
            start = (base + 1) * rows + m * piece
            initial = table[0, start : start + piece, :].astype(jnp.float32)
            mixed = ((1.0 - SHARE) * aggregate + SHARE * initial).astype(jnp.bfloat16)
            support[part, :] = mixed
            product = jnp.dot(support[part, :], slab[layer], preferred_element_type=jnp.float32)
            state = (1.0 - beta) * support[part, :].astype(jnp.float32) + beta * product
            dst[part, :] = jnp.maximum(state, 0.0).astype(jnp.bfloat16)
            done(m)

    def slab_ready(layer):
        slab_forward_half = slab.at[layer, pl.ds(core * half, half)]
        pltpu.make_async_copy(slab_forward_half, slab_forward_half, slab_land.at[layer]).wait()

        @pl.when(layer // per_section != section)
        def _():
            slab_forward(layer).start()

    def slab_swapped(layer):
        part = slab.at[layer, pl.ds((1 - core) * half, half)]
        pltpu.make_async_copy(part, part, slab_swap.at[layer]).wait()

    def project(first, last_slot):
        part = slice(first * rows, last_slot * rows)
        table[0, part, :] = jnp.maximum(
            jnp.dot(rows_in[part, :], proj[...], preferred_element_type=jnp.float32), 0.0
        ).astype(jnp.bfloat16)

    @pl.when(chain)
    def _():
        @pl.when(jnp.logical_not(inner))
        def _():
            for layer in range(1, layers):
                table[layer, at(1)] = jnp.zeros((rows, table.shape[2]), jnp.bfloat16)
            rows_in[0 : 2 * rows, :] = jnp.zeros((2 * rows, rows_in.shape[1]), jnp.bfloat16)
            ints[0:2] = jnp.zeros((2, 16, 128), jnp.int32)

        tile_load.wait()
        for n in (1, 2, 0):
            each(takes, n, lambda: int_copy(n).wait_recv())
        build(near_op, 1, 2, 1, 3)
        feature_load.wait()
        proj_load.wait()
        for n in (2, 1):
            each(takes, n, lambda: feature_copy(n).wait_recv())
        project(1, 4)
        gather(near_op, 0, 1, near_sum)
        slab_ready(0)

        def step(layer, carry):
            slab_swapped(layer)

            def send(m):
                near_copy(layer + 1, m).start()

                @pl.when((layer < layers - 2) & to_target)
                def _():
                    far_copy(layer + 1, m).start()

            propagate(near_op, layer, 1, near_sum, table.at[layer + 1, at(2)], send)

            @pl.when(lax.rem(layer + 1, per_section) == 0)
            def _():
                plane = (layer + 1) // per_section - 1
                state = table.at[layer + 1, at(2)]

                @pl.when(plane == section)
                def _():
                    out_local(state).start()

                @pl.when(plane != section)
                def _():
                    out_copy(state, plane).start()

            slab_ready(layer + 1)

            @pl.when((layer == 0) & inner)
            def _():
                feature_copy(0).wait_recv()
                project(0, 1)
                tile_copy.wait_recv()
                build(ghost_op, 0, 1, 0, 2)

            @pl.when(inner)
            def _():
                gather(ghost_op, layer, 0, ghost_sum)

            near_copy(layer + 1).wait_recv()
            gather(near_op, layer + 1, 1, near_sum)

            @pl.when((layer > 0) & inner)
            def _():
                far_copy(layer).wait_recv()

            @pl.when(inner)
            def _():
                propagate(ghost_op, layer, 0, ghost_sum, table.at[layer + 1, at(1)], lambda m: None)

            return carry

        lax.fori_loop(0, layers - 1, step, 0)
        end = layers - 1
        slab_swapped(end)

        def finish(m):
            state = last.at[pl.ds(m * piece, piece)]

            @pl.when(section == final_section)
            def _():
                out_local(state, m).start()

            @pl.when(section != final_section)
            def _():
                out_copy(state, final_section, m).start()

        propagate(near_op, end, 1, near_sum, last, finish)

        for n in range(3):
            each(gives, n, lambda: int_copy(n).wait_send())
            each(gives, n, lambda: feature_copy(n).wait_send())
        each(gives, 1, lambda: tile_copy.wait_send())
        for layer in range(1, layers):
            near_copy(layer).wait_send()
            if layer < layers - 1:
                @pl.when(to_target)
                def _():
                    far_copy(layer).wait_send()
        for layer in range(layers):
            @pl.when(layer // per_section != section)
            def _():
                slab_forward(layer).wait_send()
        for plane in range(sections):
            @pl.when(plane != section)
            def _():
                out_copy(last, plane).wait_send()
        out_local(last).wait()
        for plane in (0, 3):
            @pl.when(section == plane)
            def _():
                for copy in slab_sends(plane):
                    copy.wait_send()

        arriving = out.at[0, other_group]
        pltpu.make_async_copy(arriving, arriving, out_land.at[other_group]).wait()

    def slab_arrived(layer):
        part = slab.at[layer, pl.ds(core * half, half)]
        pltpu.make_async_copy(part, part, slab_land.at[layer]).wait()

    for plane, relayed in ((1, 5), (2, 2)):
        @pl.when(section == plane)
        def _():
            copies = slab_sends(plane)
            for (layer, to), copy in zip(routes[plane], copies):
                if layer == relayed:
                    slab_arrived(layer)
                copy.start()
            for copy in copies:
                copy.wait_send()
            for g in range(2):
                pltpu.make_async_copy(out.at[0, g], out.at[0, g], out_land.at[g]).wait()


def shards(features, input_weight, layer_weights, tiles, pub_ids, tile_src):
    groups, rows, width_in = features.shape
    width = input_weight.shape[1]
    block_total, tile_total, side = tiles.shape[1:4]
    per_section = layer_weights.shape[0]
    sections = lax.axis_size("section")
    partitions = lax.axis_size("dom")
    layers = sections * per_section
    anywhere = pl.BlockSpec(memory_space=pl.ANY)
    scalars = pl.BlockSpec(memory_space=pltpu.SMEM)
    dma = pltpu.SemaphoreType.DMA
    bf16 = jnp.bfloat16
    return pl.pallas_call(
        functools.partial(kernel, sections, partitions),
        out_shape=jax.ShapeDtypeStruct((1, groups, rows, width), bf16),
        in_specs=[anywhere] * 4 + [scalars] * 2,
        out_specs=anywhere,
        scratch_shapes=[
            pltpu.VMEM((layers, 4 * rows, width), bf16),
            pltpu.VMEM((rows, width), bf16),
            pltpu.VMEM((layers, width, width), bf16),
            pltpu.VMEM((4 * rows, width_in), bf16),
            pltpu.VMEM((width_in, width), bf16),
            pltpu.VMEM((2, block_total, tile_total, side, side), bf16),
            pltpu.VMEM((rows, 3 * rows), bf16),
            pltpu.VMEM((rows, 3 * rows), bf16),
            pltpu.VMEM((4, 16, 128), jnp.int32),
            pltpu.VMEM((rows, width), bf16),
            pltpu.VMEM((rows, width), jnp.float32),
            pltpu.VMEM((rows, width), jnp.float32),
            dma((4,)),
            dma((7,)),
            dma((4,)),
            dma((4,)),
            dma((1,)),
            dma((layers,)),
            dma((layers,)),
            dma((layers,)),
            dma((layers,)),
            dma((5,)),
            dma((layers,)),
            dma((layers,)),
            dma((layers,)),
            dma((sections,)),
            dma((groups,)),
        ],
        compiler_params=pltpu.CompilerParams(collective_id=0, has_side_effects=True),
    )(features, input_weight, layer_weights, tiles, pub_ids, tile_src)


def solution(mesh):
    in_specs = (
        P(None, "dom", None),
        P(),
        P("section", None, None),
        P(None, "dom", None, None, None),
        P(None, "dom"),
        P(None, "dom", None),
    )
    out_specs = P("section", None, "dom", None)
    return jax.shard_map(shards, mesh=mesh, in_specs=in_specs, out_specs=out_specs, check_vma=False)
```

```python
import functools
import math

import jax
import jax.numpy as jnp
from jax import lax
from jax.experimental import pallas as pl
from jax.experimental.pallas import tpu as pltpu
from jax.sharding import PartitionSpec as P

MESH = pl.DeviceIdType.MESH
SHARE = 0.1
THETA = 0.5


def remote(src, dst, sent, landed, device):
    return pltpu.make_async_remote_copy(
        src_ref=src, dst_ref=dst, send_sem=sent, recv_sem=landed, device_id=device, device_id_type=MESH
    )


def kernel(
    sections, partitions, features, input_weight, weights, tiles, pub_ids, tile_src, out,
    table, last, slab, rows_in, proj, tile_buf, near_op, ghost_op, ints, support, near_sum, ghost_sum,
    local_sem, in_sent, feat_land, int_land, tile_land, near_sent, near_land, far_sent, far_land,
    slab_sent, slab_land, slab_pass, slab_swap, out_sent, out_land,
):
    block_total, tile_total = tiles.shape[1], tiles.shape[2]
    side = tiles.shape[3]
    rows = block_total * side
    half = weights.shape[1] // 2
    per_section = weights.shape[0]
    layers = sections * per_section
    final_section = sections - 1

    section = lax.axis_index("section")
    here = lax.axis_index("dom")
    core = lax.rem(here, 2)
    outward = 2 * core - 1
    wrap = lambda q: lax.rem(q + 2 * partitions, partitions)
    mate = wrap(here + outward)
    partner = wrap(here - outward)
    source = wrap(here + 2 * outward)
    target = wrap(here - 2 * outward)
    chain = (section == 0) | (section == final_section)
    group = jnp.where(section == 0, 1, 0)
    other_group = 1 - group
    inner = (here != 0) & (here != partitions - 1)
    to_target = (target != 0) & (target != partitions - 1)
    piece = rows // 2
    at = lambda slot: pl.ds(slot * rows, rows)

    def local_half(layer, which):
        return (
            weights.at[layer - section * per_section, pl.ds(which * half, half)],
            slab.at[layer, pl.ds(which * half, half)],
        )

    feature_load = pltpu.make_async_copy(features.at[group], rows_in.at[at(2)], local_sem.at[0])
    tile_load = pltpu.make_async_copy(tiles.at[group], tile_buf.at[1], local_sem.at[1])
    proj_load = pltpu.make_async_copy(input_weight, proj, local_sem.at[2])

    @pl.when(chain)
    def _():
        feature_load.start()
        proj_load.start()
        tile_load.start()
        for i in range(per_section):
            layer = section * per_section + i
            src, dst = local_half(layer, core)
            pltpu.make_async_copy(src, dst, slab_land.at[layer]).start()
            src, dst = local_half(layer, 1 - core)
            pltpu.make_async_copy(src, dst, slab_swap.at[layer]).start()
        row = lax.broadcasted_iota(jnp.int32, (16, 128), 0)
        packed = jnp.zeros((16, 128), jnp.int32)
        for m in range(2):
            packed = jnp.where(row == m, pub_ids[group, m], packed)
        for b in range(block_total):
            for k in range(tile_total):
                packed = jnp.where(row == 2 + b * tile_total + k, tile_src[group, b, k], packed)
        ints[2] = packed

    barrier = pltpu.get_barrier_semaphore()
    def greet(device):
        pl.semaphore_signal(barrier, inc=1, device_id=device, device_id_type=MESH)

    greet((section, partner))
    for k in range(1, sections):
        greet((lax.rem(section + k, sections), here))

    @pl.when(inner)
    def _():
        greet((section, mate))
        greet((section, source))

    @pl.when(to_target)
    def _():
        greet((section, target))

    pl.semaphore_wait(barrier, sections + 2 * inner.astype(jnp.int32) + to_target.astype(jnp.int32))

    def slab_copy(n, layer, plane):
        part = pl.ds(core * half, half)
        if layer // per_section == plane_of[n]:
            src = weights.at[layer % per_section, part]
        else:
            src = slab.at[layer, part]
        return remote(src, slab.at[layer, part], slab_sent.at[n % 5], slab_land.at[layer], (plane, here))

    plane_of = [0] * 5 + [1] * 5 + [2] * 5 + [3] * 5
    routes = {
        0: ((0, 3), (1, 3)),
        1: ((2, 0), (2, 2), (3, 0), (3, 3), (5, 0)),
        2: ((4, 0), (5, 1), (2, 3), (4, 3), (5, 3)),
        3: ((6, 0), (7, 0)),
    }

    def slab_sends(plane):
        return [slab_copy(5 * plane + n, layer, to) for n, (layer, to) in enumerate(routes[plane])]

    def slab_forward(layer):
        part = slab.at[layer, pl.ds(core * half, half)]
        return remote(part, part, slab_pass.at[layer], slab_swap.at[layer], (section, partner))

    def near_copy(layer, m=None):
        src, dst = (at(2), at(3)) if m is None else (pl.ds(2 * rows + m * piece, piece), pl.ds(3 * rows + m * piece, piece))
        return remote(
            table.at[layer, src], table.at[layer, dst], near_sent.at[layer], near_land.at[layer],
            (section, partner),
        )

    def far_copy(layer, m=None):
        src, dst = (at(2), at(0)) if m is None else (pl.ds(2 * rows + m * piece, piece), pl.ds(m * piece, piece))
        return remote(
            table.at[layer, src], table.at[layer, dst], far_sent.at[layer], far_land.at[layer],
            (section, target),
        )

    def out_copy(state, plane, m=None):
        part = pl.ds(0, rows) if m is None else pl.ds(m * piece, piece)
        return remote(
            state, out.at[0, group, part], out_sent.at[plane], out_land.at[group], (plane, here)
        )

    def out_local(state, m=None):
        part = pl.ds(0, rows) if m is None else pl.ds(m * piece, piece)
        return pltpu.make_async_copy(state, out.at[0, group, part], local_sem.at[3])

    int_dests = ((0, target), (1, mate), (3, partner))

    def int_copy(n):
        slot, q = int_dests[n]
        return remote(ints.at[2], ints.at[slot], in_sent.at[n], int_land.at[slot], (section, q))

    def feature_copy(n):
        slot, q = int_dests[n]
        return remote(
            features.at[group], rows_in.at[at(slot)], in_sent.at[3 + n], feat_land.at[slot], (section, q)
        )

    tile_copy = remote(tiles.at[group], tile_buf.at[0], in_sent.at[6], tile_land.at[0], (section, mate))

    takes = (inner, inner, None)
    gives = (to_target, inner, None)

    def each(flags, n, act):
        if flags[n] is None:
            act()
        else:
            pl.when(flags[n])(act)

    @pl.when(chain)
    def _():
        for n in (1, 2, 0):
            each(gives, n, lambda: int_copy(n).start())
        for n in (1, 2, 0):
            each(gives, n, lambda: feature_copy(n).start())
        each(gives, 1, lambda: tile_copy.start())

    for plane in (0, 3):
        @pl.when(section == plane)
        def _():
            for copy in slab_sends(plane):
                copy.start()

    def build(op, tile_slot, int_slot, outer, inner):
        outer_pub = [ints[outer, m : m + 1, :] for m in range(2)]
        inner_pub = [ints[inner, m : m + 1, :] for m in range(2)]
        before = [jnp.where(core == 0, a, 4 + b) for a, b in zip(outer_pub, inner_pub)]
        after = [jnp.where(core == 0, 4 + b, a) for a, b in zip(outer_pub, inner_pub)]
        for b in range(block_total):
            columns = []
            for k in range(tile_total):
                n = 2 + b * tile_total + k
                slot = ints[int_slot, n : n + 1, :]
                column = jnp.where(slot < 2, 2 + slot, after[1])
                column = jnp.where(slot == 2, before[0], column)
                column = jnp.where(slot == 3, before[1], column)
                column = jnp.where(slot == 4, after[0], column)
                columns.append(column)
            pieces = [tile_buf[tile_slot, b, k].astype(jnp.float32) for k in range(tile_total)]
            for j in range(6):
                total = jnp.zeros((side, side), jnp.float32)
                for k in range(tile_total):
                    total += pieces[k] * (columns[k] == j).astype(jnp.float32)
                op[b * side : (b + 1) * side, j * side : (j + 1) * side] = total.astype(jnp.bfloat16)

    def gather(op, layer, base, total):
        total[...] = jnp.dot(
            op[:, rows:], table[layer, (base + 1) * rows : (base + 3) * rows, :], preferred_element_type=jnp.float32
        )

    def propagate(op, layer, base, total, dst, done):
        beta = jnp.float32(0.0)
        for i in range(layers):
            beta = jnp.where(layer == i, jnp.float32(math.log(THETA / (i + 1) + 1.0)), beta)
        for m in range(2):
            part = slice(m * piece, (m + 1) * piece)
            aggregate = total[part, :] + jnp.dot(
                op[part, :rows], table[layer, base * rows : (base + 1) * rows, :], preferred_element_type=jnp.float32
            )
            start = (base + 1) * rows + m * piece
            initial = table[0, start : start + piece, :].astype(jnp.float32)
            mixed = ((1.0 - SHARE) * aggregate + SHARE * initial).astype(jnp.bfloat16)
            support[part, :] = mixed
            product = jnp.dot(support[part, :], slab[layer], preferred_element_type=jnp.float32)
            state = (1.0 - beta) * support[part, :].astype(jnp.float32) + beta * product
            dst[part, :] = jnp.maximum(state, 0.0).astype(jnp.bfloat16)
            done(m)

    def slab_ready(layer):
        slab_forward_half = slab.at[layer, pl.ds(core * half, half)]
        pltpu.make_async_copy(slab_forward_half, slab_forward_half, slab_land.at[layer]).wait()

        @pl.when(layer // per_section != section)
        def _():
            slab_forward(layer).start()

    def slab_swapped(layer):
        part = slab.at[layer, pl.ds((1 - core) * half, half)]
        pltpu.make_async_copy(part, part, slab_swap.at[layer]).wait()

    def project(first, last_slot):
        part = slice(first * rows, last_slot * rows)
        table[0, part, :] = jnp.maximum(
            jnp.dot(rows_in[part, :], proj[...], preferred_element_type=jnp.float32), 0.0
        ).astype(jnp.bfloat16)

    @pl.when(chain)
    def _():
        @pl.when(jnp.logical_not(inner))
        def _():
            for layer in range(1, layers):
                table[layer, at(1)] = jnp.zeros((rows, table.shape[2]), jnp.bfloat16)
            rows_in[0 : 2 * rows, :] = jnp.zeros((2 * rows, rows_in.shape[1]), jnp.bfloat16)
            ints[0:2] = jnp.zeros((2, 16, 128), jnp.int32)

        tile_load.wait()
        for n in (1, 2, 0):
            each(takes, n, lambda: int_copy(n).wait_recv())
        build(near_op, 1, 2, 1, 3)
        feature_load.wait()
        proj_load.wait()
        for n in (2, 1):
            each(takes, n, lambda: feature_copy(n).wait_recv())
        project(1, 4)
        gather(near_op, 0, 1, near_sum)
        slab_ready(0)

        def step(layer, carry):
            slab_swapped(layer)

            def send(m):
                near_copy(layer + 1, m).start()

                @pl.when((layer < layers - 2) & to_target)
                def _():
                    far_copy(layer + 1, m).start()

            propagate(near_op, layer, 1, near_sum, table.at[layer + 1, at(2)], send)

            @pl.when(lax.rem(layer + 1, per_section) == 0)
            def _():
                plane = (layer + 1) // per_section - 1
                state = table.at[layer + 1, at(2)]

                @pl.when(plane == section)
                def _():
                    out_local(state).start()

                @pl.when(plane != section)
                def _():
                    out_copy(state, plane).start()

            slab_ready(layer + 1)

            @pl.when((layer == 0) & inner)
            def _():
                feature_copy(0).wait_recv()
                project(0, 1)
                tile_copy.wait_recv()
                build(ghost_op, 0, 1, 0, 2)

            @pl.when(inner)
            def _():
                gather(ghost_op, layer, 0, ghost_sum)

            near_copy(layer + 1).wait_recv()
            gather(near_op, layer + 1, 1, near_sum)

            @pl.when((layer > 0) & inner)
            def _():
                far_copy(layer).wait_recv()

            @pl.when(inner)
            def _():
                propagate(ghost_op, layer, 0, ghost_sum, table.at[layer + 1, at(1)], lambda m: None)

            return carry

        lax.fori_loop(0, layers - 1, step, 0)
        end = layers - 1
        slab_swapped(end)

        def finish(m):
            state = last.at[pl.ds(m * piece, piece)]

            @pl.when(section == final_section)
            def _():
                out_local(state, m).start()

            @pl.when(section != final_section)
            def _():
                out_copy(state, final_section, m).start()

        propagate(near_op, end, 1, near_sum, last, finish)

        for n in range(3):
            each(gives, n, lambda: int_copy(n).wait_send())
            each(gives, n, lambda: feature_copy(n).wait_send())
        each(gives, 1, lambda: tile_copy.wait_send())
        for layer in range(1, layers):
            near_copy(layer).wait_send()
            if layer < layers - 1:
                @pl.when(to_target)
                def _():
                    far_copy(layer).wait_send()
        for layer in range(layers):
            @pl.when(layer // per_section != section)
            def _():
                slab_forward(layer).wait_send()
        for plane in range(sections):
            @pl.when(plane != section)
            def _():
                out_copy(last, plane).wait_send()
        out_local(last).wait()
        for plane in (0, 3):
            @pl.when(section == plane)
            def _():
                for copy in slab_sends(plane):
                    copy.wait_send()

        arriving = out.at[0, other_group]
        pltpu.make_async_copy(arriving, arriving, out_land.at[other_group]).wait()

    def slab_arrived(layer):
        part = slab.at[layer, pl.ds(core * half, half)]
        pltpu.make_async_copy(part, part, slab_land.at[layer]).wait()

    for plane, relayed in ((1, 5), (2, 2)):
        @pl.when(section == plane)
        def _():
            copies = slab_sends(plane)
            for (layer, to), copy in zip(routes[plane], copies):
                if layer == relayed:
                    slab_arrived(layer)
                copy.start()
            for copy in copies:
                copy.wait_send()
            for g in range(2):
                pltpu.make_async_copy(out.at[0, g], out.at[0, g], out_land.at[g]).wait()


def shards(features, input_weight, layer_weights, tiles, pub_ids, tile_src):
    groups, rows, width_in = features.shape
    width = input_weight.shape[1]
    block_total, tile_total, side = tiles.shape[1:4]
    per_section = layer_weights.shape[0]
    sections = lax.axis_size("section")
    partitions = lax.axis_size("dom")
    layers = sections * per_section
    anywhere = pl.BlockSpec(memory_space=pl.ANY)
    scalars = pl.BlockSpec(memory_space=pltpu.SMEM)
    dma = pltpu.SemaphoreType.DMA
    bf16 = jnp.bfloat16
    return pl.pallas_call(
        functools.partial(kernel, sections, partitions),
        out_shape=jax.ShapeDtypeStruct((1, groups, rows, width), bf16),
        in_specs=[anywhere] * 4 + [scalars] * 2,
        out_specs=anywhere,
        scratch_shapes=[
            pltpu.VMEM((layers, 4 * rows, width), bf16),
            pltpu.VMEM((rows, width), bf16),
            pltpu.VMEM((layers, width, width), bf16),
            pltpu.VMEM((4 * rows, width_in), bf16),
            pltpu.VMEM((width_in, width), bf16),
            pltpu.VMEM((2, block_total, tile_total, side, side), bf16),
            pltpu.VMEM((rows, 3 * rows), bf16),
            pltpu.VMEM((rows, 3 * rows), bf16),
            pltpu.VMEM((4, 16, 128), jnp.int32),
            pltpu.VMEM((rows, width), bf16),
            pltpu.VMEM((rows, width), jnp.float32),
            pltpu.VMEM((rows, width), jnp.float32),
            dma((4,)),
            dma((7,)),
            dma((4,)),
            dma((4,)),
            dma((1,)),
            dma((layers,)),
            dma((layers,)),
            dma((layers,)),
            dma((layers,)),
            dma((5,)),
            dma((layers,)),
            dma((layers,)),
            dma((layers,)),
            dma((sections,)),
            dma((groups,)),
        ],
        compiler_params=pltpu.CompilerParams(collective_id=0, has_side_effects=True),
    )(features, input_weight, layer_weights, tiles, pub_ids, tile_src)


def solution(mesh):
    in_specs = (
        P(None, "dom", None),
        P(),
        P("section", None, None),
        P(None, "dom", None, None, None),
        P(None, "dom"),
        P(None, "dom", None),
    )
    out_specs = P("section", None, "dom", None)
    return jax.shard_map(shards, mesh=mesh, in_specs=in_specs, out_specs=out_specs, check_vma=False)
```

```python
import functools
import math

import jax
import jax.numpy as jnp
from jax import lax
from jax.experimental import pallas as pl
from jax.experimental.pallas import tpu as pltpu
from jax.sharding import PartitionSpec as P

MESH = pl.DeviceIdType.MESH
SHARE = 0.1
THETA = 0.5


def remote(src, dst, sent, landed, device):
    return pltpu.make_async_remote_copy(
        src_ref=src, dst_ref=dst, send_sem=sent, recv_sem=landed, device_id=device, device_id_type=MESH
    )


def kernel(
    sections, partitions, features, input_weight, weights, tiles, pub_ids, tile_src, out,
    table, last, slab, rows_in, proj, tile_buf, near_op, ghost_op, ints, support, near_sum, ghost_sum,
    local_sem, in_sent, feat_land, int_land, tile_land, near_sent, near_land, far_sent, far_land,
    slab_sent, slab_land, slab_pass, slab_swap, out_sent, out_land,
):
    block_total, tile_total = tiles.shape[1], tiles.shape[2]
    side = tiles.shape[3]
    rows = block_total * side
    half = weights.shape[1] // 2
    per_section = weights.shape[0]
    layers = sections * per_section
    final_section = sections - 1

    section = lax.axis_index("section")
    here = lax.axis_index("dom")
    core = lax.rem(here, 2)
    outward = 2 * core - 1
    wrap = lambda q: lax.rem(q + 2 * partitions, partitions)
    mate = wrap(here + outward)
    partner = wrap(here - outward)
    source = wrap(here + 2 * outward)
    target = wrap(here - 2 * outward)
    chain = (section == 0) | (section == final_section)
    group = jnp.where(section == 0, 1, 0)
    other_group = 1 - group
    inner = (here != 0) & (here != partitions - 1)
    to_target = (target != 0) & (target != partitions - 1)
    piece = rows // 2
    at = lambda slot: pl.ds(slot * rows, rows)

    def local_half(layer, which):
        return (
            weights.at[layer - section * per_section, pl.ds(which * half, half)],
            slab.at[layer, pl.ds(which * half, half)],
        )

    feature_load = pltpu.make_async_copy(features.at[group], rows_in.at[at(2)], local_sem.at[0])
    tile_load = pltpu.make_async_copy(tiles.at[group], tile_buf.at[1], local_sem.at[1])
    proj_load = pltpu.make_async_copy(input_weight, proj, local_sem.at[2])

    @pl.when(chain)
    def _():
        feature_load.start()
        proj_load.start()
        tile_load.start()
        for i in range(per_section):
            layer = section * per_section + i
            src, dst = local_half(layer, core)
            pltpu.make_async_copy(src, dst, slab_land.at[layer]).start()
            src, dst = local_half(layer, 1 - core)
            pltpu.make_async_copy(src, dst, slab_swap.at[layer]).start()
        row = lax.broadcasted_iota(jnp.int32, (16, 128), 0)
        packed = jnp.zeros((16, 128), jnp.int32)
        for m in range(2):
            packed = jnp.where(row == m, pub_ids[group, m], packed)
        for b in range(block_total):
            for k in range(tile_total):
                packed = jnp.where(row == 2 + b * tile_total + k, tile_src[group, b, k], packed)
        ints[2] = packed

    barrier = pltpu.get_barrier_semaphore()
    def greet(device):
        pl.semaphore_signal(barrier, inc=1, device_id=device, device_id_type=MESH)

    greet((section, partner))
    for k in range(1, sections):
        greet((lax.rem(section + k, sections), here))

    @pl.when(inner)
    def _():
        greet((section, mate))
        greet((section, source))

    @pl.when(to_target)
    def _():
        greet((section, target))

    pl.semaphore_wait(barrier, sections + 2 * inner.astype(jnp.int32) + to_target.astype(jnp.int32))

    def slab_copy(n, layer, plane):
        part = pl.ds(core * half, half)
        if layer // per_section == plane_of[n]:
            src = weights.at[layer % per_section, part]
        else:
            src = slab.at[layer, part]
        return remote(src, slab.at[layer, part], slab_sent.at[n % 5], slab_land.at[layer], (plane, here))

    plane_of = [0] * 5 + [1] * 5 + [2] * 5 + [3] * 5
    routes = {
        0: ((0, 3), (1, 3)),
        1: ((2, 0), (2, 2), (3, 0), (3, 2), (5, 0)),
        2: ((5, 1), (4, 0), (2, 3), (3, 3), (5, 3)),
        3: ((6, 0), (7, 0)),
    }

    def slab_sends(plane):
        return [slab_copy(5 * plane + n, layer, to) for n, (layer, to) in enumerate(routes[plane])]

    def slab_forward(layer):
        part = slab.at[layer, pl.ds(core * half, half)]
        return remote(part, part, slab_pass.at[layer], slab_swap.at[layer], (section, partner))

    def near_copy(layer, m=None):
        src, dst = (at(2), at(3)) if m is None else (pl.ds(2 * rows + m * piece, piece), pl.ds(3 * rows + m * piece, piece))
        return remote(
            table.at[layer, src], table.at[layer, dst], near_sent.at[layer], near_land.at[layer],
            (section, partner),
        )

    def far_copy(layer, m=None):
        src, dst = (at(2), at(0)) if m is None else (pl.ds(2 * rows + m * piece, piece), pl.ds(m * piece, piece))
        return remote(
            table.at[layer, src], table.at[layer, dst], far_sent.at[layer], far_land.at[layer],
            (section, target),
        )

    def out_copy(state, plane, m=None):
        part = pl.ds(0, rows) if m is None else pl.ds(m * piece, piece)
        return remote(
            state, out.at[0, group, part], out_sent.at[plane], out_land.at[group], (plane, here)
        )

    def out_local(state, m=None):
        part = pl.ds(0, rows) if m is None else pl.ds(m * piece, piece)
        return pltpu.make_async_copy(state, out.at[0, group, part], local_sem.at[3])

    int_dests = ((0, target), (1, mate), (3, partner))

    def int_copy(n):
        slot, q = int_dests[n]
        return remote(ints.at[2], ints.at[slot], in_sent.at[n], int_land.at[slot], (section, q))

    def feature_copy(n):
        slot, q = int_dests[n]
        return remote(
            features.at[group], rows_in.at[at(slot)], in_sent.at[3 + n], feat_land.at[slot], (section, q)
        )

    tile_copy = remote(tiles.at[group], tile_buf.at[0], in_sent.at[6], tile_land.at[0], (section, mate))

    takes = (inner, inner, None)
    gives = (to_target, inner, None)

    def each(flags, n, act):
        if flags[n] is None:
            act()
        else:
            pl.when(flags[n])(act)

    @pl.when(chain)
    def _():
        for n in (1, 2, 0):
            each(gives, n, lambda: int_copy(n).start())
        for n in (1, 2, 0):
            each(gives, n, lambda: feature_copy(n).start())
        each(gives, 1, lambda: tile_copy.start())

    for plane in (0, 3):
        @pl.when(section == plane)
        def _():
            for copy in slab_sends(plane):
                copy.start()

    def build(op, tile_slot, int_slot, outer, inner):
        outer_pub = [ints[outer, m : m + 1, :] for m in range(2)]
        inner_pub = [ints[inner, m : m + 1, :] for m in range(2)]
        before = [jnp.where(core == 0, a, 4 + b) for a, b in zip(outer_pub, inner_pub)]
        after = [jnp.where(core == 0, 4 + b, a) for a, b in zip(outer_pub, inner_pub)]
        for b in range(block_total):
            columns = []
            for k in range(tile_total):
                n = 2 + b * tile_total + k
                slot = ints[int_slot, n : n + 1, :]
                column = jnp.where(slot < 2, 2 + slot, after[1])
                column = jnp.where(slot == 2, before[0], column)
                column = jnp.where(slot == 3, before[1], column)
                column = jnp.where(slot == 4, after[0], column)
                columns.append(column)
            pieces = [tile_buf[tile_slot, b, k].astype(jnp.float32) for k in range(tile_total)]
            for j in range(6):
                total = jnp.zeros((side, side), jnp.float32)
                for k in range(tile_total):
                    total += pieces[k] * (columns[k] == j).astype(jnp.float32)
                op[b * side : (b + 1) * side, j * side : (j + 1) * side] = total.astype(jnp.bfloat16)

    def gather(op, layer, base, total):
        total[...] = jnp.dot(
            op[:, rows:], table[layer, (base + 1) * rows : (base + 3) * rows, :], preferred_element_type=jnp.float32
        )

    def propagate(op, layer, base, total, dst, done):
        beta = jnp.float32(0.0)
        for i in range(layers):
            beta = jnp.where(layer == i, jnp.float32(math.log(THETA / (i + 1) + 1.0)), beta)
        for m in range(2):
            part = slice(m * piece, (m + 1) * piece)
            aggregate = total[part, :] + jnp.dot(
                op[part, :rows], table[layer, base * rows : (base + 1) * rows, :], preferred_element_type=jnp.float32
            )
            start = (base + 1) * rows + m * piece
            initial = table[0, start : start + piece, :].astype(jnp.float32)
            mixed = ((1.0 - SHARE) * aggregate + SHARE * initial).astype(jnp.bfloat16)
            support[part, :] = mixed
            product = jnp.dot(support[part, :], slab[layer], preferred_element_type=jnp.float32)
            state = (1.0 - beta) * support[part, :].astype(jnp.float32) + beta * product
            dst[part, :] = jnp.maximum(state, 0.0).astype(jnp.bfloat16)
            done(m)

    def slab_ready(layer):
        slab_forward_half = slab.at[layer, pl.ds(core * half, half)]
        pltpu.make_async_copy(slab_forward_half, slab_forward_half, slab_land.at[layer]).wait()

        @pl.when(layer // per_section != section)
        def _():
            slab_forward(layer).start()

        @pl.when((layer == 4) & (section == 0))
        def _():
            slab_copy(4, 4, 3).start()

    def slab_swapped(layer):
        part = slab.at[layer, pl.ds((1 - core) * half, half)]
        pltpu.make_async_copy(part, part, slab_swap.at[layer]).wait()

    def project(first, last_slot):
        part = slice(first * rows, last_slot * rows)
        table[0, part, :] = jnp.maximum(
            jnp.dot(rows_in[part, :], proj[...], preferred_element_type=jnp.float32), 0.0
        ).astype(jnp.bfloat16)

    @pl.when(chain)
    def _():
        @pl.when(jnp.logical_not(inner))
        def _():
            for layer in range(1, layers):
                table[layer, at(1)] = jnp.zeros((rows, table.shape[2]), jnp.bfloat16)
            rows_in[0 : 2 * rows, :] = jnp.zeros((2 * rows, rows_in.shape[1]), jnp.bfloat16)
            ints[0:2] = jnp.zeros((2, 16, 128), jnp.int32)

        tile_load.wait()
        for n in (1, 2, 0):
            each(takes, n, lambda: int_copy(n).wait_recv())
        build(near_op, 1, 2, 1, 3)
        feature_load.wait()
        proj_load.wait()
        for n in (2, 1):
            each(takes, n, lambda: feature_copy(n).wait_recv())
        project(1, 4)
        gather(near_op, 0, 1, near_sum)
        slab_ready(0)

        def step(layer, carry):
            slab_swapped(layer)

            def send(m):
                near_copy(layer + 1, m).start()

                @pl.when((layer < layers - 2) & to_target)
                def _():
                    far_copy(layer + 1, m).start()

            propagate(near_op, layer, 1, near_sum, table.at[layer + 1, at(2)], send)

            @pl.when(lax.rem(layer + 1, per_section) == 0)
            def _():
                plane = (layer + 1) // per_section - 1
                state = table.at[layer + 1, at(2)]

                @pl.when(plane == section)
                def _():
                    out_local(state).start()

                @pl.when(plane != section)
                def _():
                    out_copy(state, plane).start()

            slab_ready(layer + 1)

            @pl.when((layer == 0) & inner)
            def _():
                feature_copy(0).wait_recv()
                project(0, 1)
                tile_copy.wait_recv()
                build(ghost_op, 0, 1, 0, 2)

            @pl.when(inner)
            def _():
                gather(ghost_op, layer, 0, ghost_sum)

            near_copy(layer + 1).wait_recv()
            gather(near_op, layer + 1, 1, near_sum)

            @pl.when((layer > 0) & inner)
            def _():
                far_copy(layer).wait_recv()

            @pl.when(inner)
            def _():
                propagate(ghost_op, layer, 0, ghost_sum, table.at[layer + 1, at(1)], lambda m: None)

            return carry

        lax.fori_loop(0, layers - 1, step, 0)
        end = layers - 1
        slab_swapped(end)

        def finish(m):
            state = last.at[pl.ds(m * piece, piece)]

            @pl.when(section == final_section)
            def _():
                out_local(state, m).start()

            @pl.when(section != final_section)
            def _():
                out_copy(state, final_section, m).start()

        propagate(near_op, end, 1, near_sum, last, finish)

        for n in range(3):
            each(gives, n, lambda: int_copy(n).wait_send())
            each(gives, n, lambda: feature_copy(n).wait_send())
        each(gives, 1, lambda: tile_copy.wait_send())
        for layer in range(1, layers):
            near_copy(layer).wait_send()
            if layer < layers - 1:
                @pl.when(to_target)
                def _():
                    far_copy(layer).wait_send()
        for layer in range(layers):
            @pl.when(layer // per_section != section)
            def _():
                slab_forward(layer).wait_send()
        for plane in range(sections):
            @pl.when(plane != section)
            def _():
                out_copy(last, plane).wait_send()
        out_local(last).wait()
        for plane in (0, 3):
            @pl.when(section == plane)
            def _():
                for copy in slab_sends(plane):
                    copy.wait_send()

        @pl.when(section == 0)
        def _():
            slab_copy(4, 4, 3).wait_send()

        arriving = out.at[0, other_group]
        pltpu.make_async_copy(arriving, arriving, out_land.at[other_group]).wait()

    def slab_arrived(layer):
        part = slab.at[layer, pl.ds(core * half, half)]
        pltpu.make_async_copy(part, part, slab_land.at[layer]).wait()

    for plane in (1, 2):
        @pl.when(section == plane)
        def _():
            copies = slab_sends(plane)
            for (layer, to), copy in zip(routes[plane], copies):
                if layer // per_section != plane:
                    slab_arrived(layer)
                copy.start()
            for copy in copies:
                copy.wait_send()
            for g in range(2):
                pltpu.make_async_copy(out.at[0, g], out.at[0, g], out_land.at[g]).wait()


def shards(features, input_weight, layer_weights, tiles, pub_ids, tile_src):
    groups, rows, width_in = features.shape
    width = input_weight.shape[1]
    block_total, tile_total, side = tiles.shape[1:4]
    per_section = layer_weights.shape[0]
    sections = lax.axis_size("section")
    partitions = lax.axis_size("dom")
    layers = sections * per_section
    anywhere = pl.BlockSpec(memory_space=pl.ANY)
    scalars = pl.BlockSpec(memory_space=pltpu.SMEM)
    dma = pltpu.SemaphoreType.DMA
    bf16 = jnp.bfloat16
    return pl.pallas_call(
        functools.partial(kernel, sections, partitions),
        out_shape=jax.ShapeDtypeStruct((1, groups, rows, width), bf16),
        in_specs=[anywhere] * 4 + [scalars] * 2,
        out_specs=anywhere,
        scratch_shapes=[
            pltpu.VMEM((layers, 4 * rows, width), bf16),
            pltpu.VMEM((rows, width), bf16),
            pltpu.VMEM((layers, width, width), bf16),
            pltpu.VMEM((4 * rows, width_in), bf16),
            pltpu.VMEM((width_in, width), bf16),
            pltpu.VMEM((2, block_total, tile_total, side, side), bf16),
            pltpu.VMEM((rows, 3 * rows), bf16),
            pltpu.VMEM((rows, 3 * rows), bf16),
            pltpu.VMEM((4, 16, 128), jnp.int32),
            pltpu.VMEM((rows, width), bf16),
            pltpu.VMEM((rows, width), jnp.float32),
            pltpu.VMEM((rows, width), jnp.float32),
            dma((4,)),
            dma((7,)),
            dma((4,)),
            dma((4,)),
            dma((1,)),
            dma((layers,)),
            dma((layers,)),
            dma((layers,)),
            dma((layers,)),
            dma((5,)),
            dma((layers,)),
            dma((layers,)),
            dma((layers,)),
            dma((sections,)),
            dma((groups,)),
        ],
        compiler_params=pltpu.CompilerParams(collective_id=0, has_side_effects=True),
    )(features, input_weight, layer_weights, tiles, pub_ids, tile_src)


def solution(mesh):
    in_specs = (
        P(None, "dom", None),
        P(),
        P("section", None, None),
        P(None, "dom", None, None, None),
        P(None, "dom"),
        P(None, "dom", None),
    )
    out_specs = P("section", None, "dom", None)
    return jax.shard_map(shards, mesh=mesh, in_specs=in_specs, out_specs=out_specs, check_vma=False)
```

```python
import functools
import math

import jax
import jax.numpy as jnp
from jax import lax
from jax.experimental import pallas as pl
from jax.experimental.pallas import tpu as pltpu
from jax.sharding import PartitionSpec as P

MESH = pl.DeviceIdType.MESH
SHARE = 0.1
THETA = 0.5


def remote(src, dst, sent, landed, device):
    return pltpu.make_async_remote_copy(
        src_ref=src, dst_ref=dst, send_sem=sent, recv_sem=landed, device_id=device, device_id_type=MESH
    )


def kernel(
    sections, partitions, features, input_weight, weights, tiles, pub_array, src_array, out,
    pub_ids, tile_src, table, last, slab, rows_in, proj, tile_buf, near_op, ghost_op, ints, support, near_sum, ghost_sum,
    local_sem, in_sent, feat_land, int_land, tile_land, near_sent, near_land, far_sent, far_land,
    slab_sent, slab_land, slab_pass, slab_swap, out_sent, out_land,
):
    block_total, tile_total = tiles.shape[1], tiles.shape[2]
    side = tiles.shape[3]
    rows = block_total * side
    half = weights.shape[1] // 2
    per_section = weights.shape[0]
    layers = sections * per_section
    final_section = sections - 1

    section = lax.axis_index("section")
    here = lax.axis_index("dom")
    core = lax.rem(here, 2)
    outward = 2 * core - 1
    wrap = lambda q: lax.rem(q + 2 * partitions, partitions)
    mate = wrap(here + outward)
    partner = wrap(here - outward)
    source = wrap(here + 2 * outward)
    target = wrap(here - 2 * outward)
    chain = (section == 0) | (section == final_section)
    group = jnp.where(section == 0, 1, 0)
    other_group = 1 - group
    inner = (here != 0) & (here != partitions - 1)
    to_target = (target != 0) & (target != partitions - 1)
    piece = rows // 2
    at = lambda slot: pl.ds(slot * rows, rows)

    def local_half(layer, which):
        return (
            weights.at[layer - section * per_section, pl.ds(which * half, half)],
            slab.at[layer, pl.ds(which * half, half)],
        )

    feature_load = pltpu.make_async_copy(features.at[group], rows_in.at[at(2)], local_sem.at[0])
    tile_load = pltpu.make_async_copy(tiles.at[group], tile_buf.at[1], local_sem.at[1])
    proj_load = pltpu.make_async_copy(input_weight, proj, local_sem.at[2])

    scalar_loads = (
        pltpu.make_async_copy(pub_array, pub_ids, local_sem.at[4]),
        pltpu.make_async_copy(src_array, tile_src, local_sem.at[5]),
    )

    @pl.when(chain)
    def _():
        for copy in scalar_loads:
            copy.start()
        feature_load.start()
        proj_load.start()
        tile_load.start()
        for i in range(per_section):
            layer = section * per_section + i
            src, dst = local_half(layer, core)
            pltpu.make_async_copy(src, dst, slab_land.at[layer]).start()
            src, dst = local_half(layer, 1 - core)
            pltpu.make_async_copy(src, dst, slab_swap.at[layer]).start()
        for copy in scalar_loads:
            copy.wait()
        row = lax.broadcasted_iota(jnp.int32, (16, 128), 0)
        packed = jnp.zeros((16, 128), jnp.int32)
        for m in range(2):
            packed = jnp.where(row == m, pub_ids[group, m], packed)
        for b in range(block_total):
            for k in range(tile_total):
                packed = jnp.where(row == 2 + b * tile_total + k, tile_src[group, b, k], packed)
        ints[2] = packed

    barrier = pltpu.get_barrier_semaphore()
    def greet(device):
        pl.semaphore_signal(barrier, inc=1, device_id=device, device_id_type=MESH)

    greet((section, partner))
    for k in range(1, sections):
        greet((lax.rem(section + k, sections), here))

    @pl.when(inner)
    def _():
        greet((section, mate))
        greet((section, source))

    @pl.when(to_target)
    def _():
        greet((section, target))

    pl.semaphore_wait(barrier, sections + 2 * inner.astype(jnp.int32) + to_target.astype(jnp.int32))

    def slab_copy(n, layer, plane):
        part = pl.ds(core * half, half)
        if layer // per_section == plane_of[n]:
            src = weights.at[layer % per_section, part]
        else:
            src = slab.at[layer, part]
        return remote(src, slab.at[layer, part], slab_sent.at[n % 5], slab_land.at[layer], (plane, here))

    plane_of = [0] * 5 + [1] * 5 + [2] * 5 + [3] * 5
    routes = {
        0: ((0, 3), (1, 3)),
        1: ((2, 0), (2, 2), (3, 0), (3, 2), (5, 0)),
        2: ((5, 1), (4, 0), (2, 3), (3, 3), (5, 3)),
        3: ((6, 0), (7, 0)),
    }

    def slab_sends(plane):
        return [slab_copy(5 * plane + n, layer, to) for n, (layer, to) in enumerate(routes[plane])]

    def slab_forward(layer):
        part = slab.at[layer, pl.ds(core * half, half)]
        return remote(part, part, slab_pass.at[layer], slab_swap.at[layer], (section, partner))

    def near_copy(layer, m=None):
        src, dst = (at(2), at(3)) if m is None else (pl.ds(2 * rows + m * piece, piece), pl.ds(3 * rows + m * piece, piece))
        return remote(
            table.at[layer, src], table.at[layer, dst], near_sent.at[layer], near_land.at[layer],
            (section, partner),
        )

    def far_copy(layer, m=None):
        src, dst = (at(2), at(0)) if m is None else (pl.ds(2 * rows + m * piece, piece), pl.ds(m * piece, piece))
        return remote(
            table.at[layer, src], table.at[layer, dst], far_sent.at[layer], far_land.at[layer],
            (section, target),
        )

    def out_copy(state, plane, m=None):
        part = pl.ds(0, rows) if m is None else pl.ds(m * piece, piece)
        return remote(
            state, out.at[0, group, part], out_sent.at[plane], out_land.at[group], (plane, here)
        )

    def out_local(state, m=None):
        part = pl.ds(0, rows) if m is None else pl.ds(m * piece, piece)
        return pltpu.make_async_copy(state, out.at[0, group, part], local_sem.at[3])

    int_dests = ((0, target), (1, mate), (3, partner))

    def int_copy(n):
        slot, q = int_dests[n]
        return remote(ints.at[2], ints.at[slot], in_sent.at[n], int_land.at[slot], (section, q))

    def feature_copy(n):
        slot, q = int_dests[n]
        return remote(
            features.at[group], rows_in.at[at(slot)], in_sent.at[3 + n], feat_land.at[slot], (section, q)
        )

    tile_copy = remote(tiles.at[group], tile_buf.at[0], in_sent.at[6], tile_land.at[0], (section, mate))

    takes = (inner, inner, None)
    gives = (to_target, inner, None)

    def each(flags, n, act):
        if flags[n] is None:
            act()
        else:
            pl.when(flags[n])(act)

    @pl.when(chain)
    def _():
        for n in (1, 2, 0):
            each(gives, n, lambda: int_copy(n).start())
        for n in (1, 2, 0):
            each(gives, n, lambda: feature_copy(n).start())
        each(gives, 1, lambda: tile_copy.start())

    for plane in (0, 3):
        @pl.when(section == plane)
        def _():
            for copy in slab_sends(plane):
                copy.start()

    def build(op, tile_slot, int_slot, outer, inner):
        outer_pub = [ints[outer, m : m + 1, :] for m in range(2)]
        inner_pub = [ints[inner, m : m + 1, :] for m in range(2)]
        before = [jnp.where(core == 0, a, 4 + b) for a, b in zip(outer_pub, inner_pub)]
        after = [jnp.where(core == 0, 4 + b, a) for a, b in zip(outer_pub, inner_pub)]
        for b in range(block_total):
            columns = []
            for k in range(tile_total):
                n = 2 + b * tile_total + k
                slot = ints[int_slot, n : n + 1, :]
                column = jnp.where(slot < 2, 2 + slot, after[1])
                column = jnp.where(slot == 2, before[0], column)
                column = jnp.where(slot == 3, before[1], column)
                column = jnp.where(slot == 4, after[0], column)
                columns.append(column)
            pieces = [tile_buf[tile_slot, b, k].astype(jnp.float32) for k in range(tile_total)]
            for j in range(6):
                total = jnp.zeros((side, side), jnp.float32)
                for k in range(tile_total):
                    total += pieces[k] * (columns[k] == j).astype(jnp.float32)
                op[b * side : (b + 1) * side, j * side : (j + 1) * side] = total.astype(jnp.bfloat16)

    def gather(op, layer, base, total):
        total[...] = jnp.dot(
            op[:, rows:], table[layer, (base + 1) * rows : (base + 3) * rows, :], preferred_element_type=jnp.float32
        )

    def propagate(op, layer, base, total, dst, done):
        beta = jnp.float32(0.0)
        for i in range(layers):
            beta = jnp.where(layer == i, jnp.float32(math.log(THETA / (i + 1) + 1.0)), beta)
        for m in range(2):
            part = slice(m * piece, (m + 1) * piece)
            aggregate = total[part, :] + jnp.dot(
                op[part, :rows], table[layer, base * rows : (base + 1) * rows, :], preferred_element_type=jnp.float32
            )
            start = (base + 1) * rows + m * piece
            initial = table[0, start : start + piece, :].astype(jnp.float32)
            mixed = ((1.0 - SHARE) * aggregate + SHARE * initial).astype(jnp.bfloat16)
            support[part, :] = mixed
            product = jnp.dot(support[part, :], slab[layer], preferred_element_type=jnp.float32)
            state = (1.0 - beta) * support[part, :].astype(jnp.float32) + beta * product
            dst[part, :] = jnp.maximum(state, 0.0).astype(jnp.bfloat16)
            done(m)

    def slab_ready(layer):
        slab_forward_half = slab.at[layer, pl.ds(core * half, half)]
        pltpu.make_async_copy(slab_forward_half, slab_forward_half, slab_land.at[layer]).wait()

        @pl.when(layer // per_section != section)
        def _():
            slab_forward(layer).start()

        @pl.when((layer == 4) & (section == 0))
        def _():
            slab_copy(4, 4, 3).start()

    def slab_swapped(layer):
        part = slab.at[layer, pl.ds((1 - core) * half, half)]
        pltpu.make_async_copy(part, part, slab_swap.at[layer]).wait()

    def project(first, last_slot):
        part = slice(first * rows, last_slot * rows)
        table[0, part, :] = jnp.maximum(
            jnp.dot(rows_in[part, :], proj[...], preferred_element_type=jnp.float32), 0.0
        ).astype(jnp.bfloat16)

    @pl.when(chain)
    def _():
        @pl.when(jnp.logical_not(inner))
        def _():
            for layer in range(1, layers):
                table[layer, at(1)] = jnp.zeros((rows, table.shape[2]), jnp.bfloat16)
            rows_in[0 : 2 * rows, :] = jnp.zeros((2 * rows, rows_in.shape[1]), jnp.bfloat16)
            ints[0:2] = jnp.zeros((2, 16, 128), jnp.int32)

        tile_load.wait()
        for n in (1, 2, 0):
            each(takes, n, lambda: int_copy(n).wait_recv())
        build(near_op, 1, 2, 1, 3)
        feature_load.wait()
        proj_load.wait()
        for n in (2, 1):
            each(takes, n, lambda: feature_copy(n).wait_recv())
        project(1, 4)
        gather(near_op, 0, 1, near_sum)
        slab_ready(0)

        def step(layer, carry):
            slab_swapped(layer)

            def send(m):
                near_copy(layer + 1, m).start()

                @pl.when((layer < layers - 2) & to_target)
                def _():
                    far_copy(layer + 1, m).start()

            propagate(near_op, layer, 1, near_sum, table.at[layer + 1, at(2)], send)

            @pl.when(lax.rem(layer + 1, per_section) == 0)
            def _():
                plane = (layer + 1) // per_section - 1
                state = table.at[layer + 1, at(2)]

                @pl.when(plane == section)
                def _():
                    out_local(state).start()

                @pl.when(plane != section)
                def _():
                    out_copy(state, plane).start()

            slab_ready(layer + 1)

            @pl.when((layer == 0) & inner)
            def _():
                feature_copy(0).wait_recv()
                project(0, 1)
                tile_copy.wait_recv()
                build(ghost_op, 0, 1, 0, 2)

            @pl.when(inner)
            def _():
                gather(ghost_op, layer, 0, ghost_sum)

            near_copy(layer + 1).wait_recv()
            gather(near_op, layer + 1, 1, near_sum)

            @pl.when((layer > 0) & inner)
            def _():
                far_copy(layer).wait_recv()

            @pl.when(inner)
            def _():
                propagate(ghost_op, layer, 0, ghost_sum, table.at[layer + 1, at(1)], lambda m: None)

            return carry

        lax.fori_loop(0, layers - 1, step, 0)
        end = layers - 1
        slab_swapped(end)

        def finish(m):
            state = last.at[pl.ds(m * piece, piece)]

            @pl.when(section == final_section)
            def _():
                out_local(state, m).start()

            @pl.when(section != final_section)
            def _():
                out_copy(state, final_section, m).start()

        propagate(near_op, end, 1, near_sum, last, finish)

        for n in range(3):
            each(gives, n, lambda: int_copy(n).wait_send())
            each(gives, n, lambda: feature_copy(n).wait_send())
        each(gives, 1, lambda: tile_copy.wait_send())
        for layer in range(1, layers):
            near_copy(layer).wait_send()
            if layer < layers - 1:
                @pl.when(to_target)
                def _():
                    far_copy(layer).wait_send()
        for layer in range(layers):
            @pl.when(layer // per_section != section)
            def _():
                slab_forward(layer).wait_send()
        for plane in range(sections):
            @pl.when(plane != section)
            def _():
                out_copy(last, plane).wait_send()
        out_local(last).wait()
        for plane in (0, 3):
            @pl.when(section == plane)
            def _():
                for copy in slab_sends(plane):
                    copy.wait_send()

        @pl.when(section == 0)
        def _():
            slab_copy(4, 4, 3).wait_send()

        arriving = out.at[0, other_group]
        pltpu.make_async_copy(arriving, arriving, out_land.at[other_group]).wait()

    def slab_arrived(layer):
        part = slab.at[layer, pl.ds(core * half, half)]
        pltpu.make_async_copy(part, part, slab_land.at[layer]).wait()

    for plane in (1, 2):
        @pl.when(section == plane)
        def _():
            copies = slab_sends(plane)
            for (layer, to), copy in zip(routes[plane], copies):
                if layer // per_section != plane:
                    slab_arrived(layer)
                copy.start()
            for copy in copies:
                copy.wait_send()
            for g in range(2):
                pltpu.make_async_copy(out.at[0, g], out.at[0, g], out_land.at[g]).wait()


def shards(features, input_weight, layer_weights, tiles, pub_ids, tile_src):
    groups, rows, width_in = features.shape
    width = input_weight.shape[1]
    block_total, tile_total, side = tiles.shape[1:4]
    per_section = layer_weights.shape[0]
    sections = lax.axis_size("section")
    partitions = lax.axis_size("dom")
    layers = sections * per_section
    anywhere = pl.BlockSpec(memory_space=pl.ANY)
    dma = pltpu.SemaphoreType.DMA
    bf16 = jnp.bfloat16
    held = [
        pltpu.with_memory_space_constraint(value, pltpu.HBM)
        for value in (features, input_weight, layer_weights, tiles, pub_ids, tile_src)
    ]
    return pl.pallas_call(
        functools.partial(kernel, sections, partitions),
        out_shape=jax.ShapeDtypeStruct((1, groups, rows, width), bf16),
        in_specs=[anywhere] * 6,
        out_specs=anywhere,
        scratch_shapes=[
            pltpu.SMEM(pub_ids.shape, jnp.int32),
            pltpu.SMEM(tile_src.shape, jnp.int32),
            pltpu.VMEM((layers, 4 * rows, width), bf16),
            pltpu.VMEM((rows, width), bf16),
            pltpu.VMEM((layers, width, width), bf16),
            pltpu.VMEM((4 * rows, width_in), bf16),
            pltpu.VMEM((width_in, width), bf16),
            pltpu.VMEM((2, block_total, tile_total, side, side), bf16),
            pltpu.VMEM((rows, 3 * rows), bf16),
            pltpu.VMEM((rows, 3 * rows), bf16),
            pltpu.VMEM((4, 16, 128), jnp.int32),
            pltpu.VMEM((rows, width), bf16),
            pltpu.VMEM((rows, width), jnp.float32),
            pltpu.VMEM((rows, width), jnp.float32),
            dma((6,)),
            dma((7,)),
            dma((4,)),
            dma((4,)),
            dma((1,)),
            dma((layers,)),
            dma((layers,)),
            dma((layers,)),
            dma((layers,)),
            dma((5,)),
            dma((layers,)),
            dma((layers,)),
            dma((layers,)),
            dma((sections,)),
            dma((groups,)),
        ],
        compiler_params=pltpu.CompilerParams(collective_id=0, has_side_effects=True, vmem_limit_bytes=40 * 2**20),
    )(*held)


def solution(mesh):
    in_specs = (
        P(None, "dom", None),
        P(),
        P("section", None, None),
        P(None, "dom", None, None, None),
        P(None, "dom"),
        P(None, "dom", None),
    )
    out_specs = P("section", None, "dom", None)
    return jax.shard_map(shards, mesh=mesh, in_specs=in_specs, out_specs=out_specs, check_vma=False)
```

```python
import functools
import math

import jax
import jax.numpy as jnp
from jax import lax
from jax.experimental import pallas as pl
from jax.experimental.pallas import tpu as pltpu
from jax.sharding import PartitionSpec as P

MESH = pl.DeviceIdType.MESH
SHARE = 0.1
THETA = 0.5


def remote(src, dst, sent, landed, device):
    return pltpu.make_async_remote_copy(
        src_ref=src, dst_ref=dst, send_sem=sent, recv_sem=landed, device_id=device, device_id_type=MESH
    )


def kernel(
    sections, partitions, features, input_weight, weights, tiles, pub_array, src_array, out,
    pub_ids, tile_src, table, last, slab, rows_in, proj, tile_buf, near_op, ghost_op, ints, support, near_sum, ghost_sum,
    local_sem, in_sent, feat_land, int_land, tile_land, near_sent, near_land, far_sent, far_land,
    slab_sent, slab_land, slab_pass, slab_swap, out_sent, out_land,
):
    block_total, tile_total = tiles.shape[1], tiles.shape[2]
    side = tiles.shape[3]
    rows = block_total * side
    half = weights.shape[1] // 2
    per_section = weights.shape[0]
    layers = sections * per_section
    final_section = sections - 1

    section = lax.axis_index("section")
    here = lax.axis_index("dom")
    core = lax.rem(here, 2)
    outward = 2 * core - 1
    wrap = lambda q: lax.rem(q + 2 * partitions, partitions)
    mate = wrap(here + outward)
    partner = wrap(here - outward)
    source = wrap(here + 2 * outward)
    target = wrap(here - 2 * outward)
    chain = (section == 0) | (section == final_section)
    group = jnp.where(section == 0, 1, 0)
    other_group = 1 - group
    inner = (here != 0) & (here != partitions - 1)
    to_target = (target != 0) & (target != partitions - 1)
    piece = rows // 2
    at = lambda slot: pl.ds(slot * rows, rows)

    def local_half(layer, which):
        return (
            weights.at[layer - section * per_section, pl.ds(which * half, half)],
            slab.at[layer, pl.ds(which * half, half)],
        )

    feature_load = pltpu.make_async_copy(features.at[group], rows_in.at[at(2)], local_sem.at[0])
    tile_load = pltpu.make_async_copy(tiles.at[group], tile_buf.at[1], local_sem.at[1])
    proj_load = pltpu.make_async_copy(input_weight, proj, local_sem.at[2])

    scalar_loads = (
        pltpu.make_async_copy(pub_array, pub_ids, local_sem.at[4]),
        pltpu.make_async_copy(src_array, tile_src, local_sem.at[5]),
    )

    @pl.when(chain)
    def _():
        for copy in scalar_loads:
            copy.start()
        feature_load.start()
        proj_load.start()
        tile_load.start()
        for i in range(per_section):
            layer = section * per_section + i
            src, dst = local_half(layer, core)
            pltpu.make_async_copy(src, dst, slab_land.at[layer]).start()
            src, dst = local_half(layer, 1 - core)
            pltpu.make_async_copy(src, dst, slab_swap.at[layer]).start()
        for copy in scalar_loads:
            copy.wait()
        row = lax.broadcasted_iota(jnp.int32, (16, 128), 0)
        packed = jnp.zeros((16, 128), jnp.int32)
        for m in range(2):
            packed = jnp.where(row == m, pub_ids[group, m], packed)
        for b in range(block_total):
            for k in range(tile_total):
                packed = jnp.where(row == 2 + b * tile_total + k, tile_src[group, b, k], packed)
        ints[2] = packed

    barrier = pltpu.get_barrier_semaphore()
    def greet(device):
        pl.semaphore_signal(barrier, inc=1, device_id=device, device_id_type=MESH)

    greet((section, partner))
    for k in range(1, sections):
        greet((lax.rem(section + k, sections), here))

    @pl.when(inner)
    def _():
        greet((section, mate))
        greet((section, source))

    @pl.when(to_target)
    def _():
        greet((section, target))

    pl.semaphore_wait(barrier, sections + 2 * inner.astype(jnp.int32) + to_target.astype(jnp.int32))

    def slab_copy(n, layer, plane):
        part = pl.ds(core * half, half)
        if layer // per_section == plane_of[n]:
            src = weights.at[layer % per_section, part]
        else:
            src = slab.at[layer, part]
        return remote(src, slab.at[layer, part], slab_sent.at[n % 5], slab_land.at[layer], (plane, here))

    plane_of = [0] * 5 + [1] * 5 + [2] * 5 + [3] * 5
    routes = {
        0: ((0, 3), (1, 3)),
        1: ((2, 0), (2, 2), (3, 0), (3, 2), (5, 0)),
        2: ((5, 1), (4, 0), (2, 3), (3, 3), (5, 3)),
        3: ((6, 0), (7, 0)),
    }

    def slab_sends(plane):
        return [slab_copy(5 * plane + n, layer, to) for n, (layer, to) in enumerate(routes[plane])]

    def slab_forward(layer):
        part = slab.at[layer, pl.ds(core * half, half)]
        return remote(part, part, slab_pass.at[layer], slab_swap.at[layer], (section, partner))

    def near_copy(layer, m=None):
        src, dst = (at(2), at(3)) if m is None else (pl.ds(2 * rows + m * piece, piece), pl.ds(3 * rows + m * piece, piece))
        return remote(
            table.at[layer, src], table.at[layer, dst], near_sent.at[layer], near_land.at[layer],
            (section, partner),
        )

    def far_copy(layer, m=None):
        src, dst = (at(2), at(0)) if m is None else (pl.ds(2 * rows + m * piece, piece), pl.ds(m * piece, piece))
        return remote(
            table.at[layer, src], table.at[layer, dst], far_sent.at[layer], far_land.at[layer],
            (section, target),
        )

    def out_copy(state, plane, m=None):
        part = pl.ds(0, rows) if m is None else pl.ds(m * piece, piece)
        return remote(
            state, out.at[0, group, part], out_sent.at[plane], out_land.at[group], (plane, here)
        )

    def out_local(state, m=None):
        part = pl.ds(0, rows) if m is None else pl.ds(m * piece, piece)
        return pltpu.make_async_copy(state, out.at[0, group, part], local_sem.at[3])

    int_dests = ((0, target), (1, mate), (3, partner))

    def int_copy(n):
        slot, q = int_dests[n]
        return remote(ints.at[2], ints.at[slot], in_sent.at[n], int_land.at[slot], (section, q))

    def feature_copy(n):
        slot, q = int_dests[n]
        return remote(
            features.at[group], rows_in.at[at(slot)], in_sent.at[3 + n], feat_land.at[slot], (section, q)
        )

    tile_copy = remote(tiles.at[group], tile_buf.at[0], in_sent.at[6], tile_land.at[0], (section, mate))

    takes = (inner, inner, None)
    gives = (to_target, inner, None)

    def each(flags, n, act):
        if flags[n] is None:
            act()
        else:
            pl.when(flags[n])(act)

    @pl.when(chain)
    def _():
        for n in (1, 2, 0):
            each(gives, n, lambda: int_copy(n).start())
        for n in (1, 2, 0):
            each(gives, n, lambda: feature_copy(n).start())
        each(gives, 1, lambda: tile_copy.start())

    for plane in (0, 3):
        @pl.when(section == plane)
        def _():
            for copy in slab_sends(plane):
                copy.start()

    def build(op, tile_slot, int_slot, outer, inner):
        outer_pub = [ints[outer, m : m + 1, :] for m in range(2)]
        inner_pub = [ints[inner, m : m + 1, :] for m in range(2)]
        before = [jnp.where(core == 0, a, 4 + b) for a, b in zip(outer_pub, inner_pub)]
        after = [jnp.where(core == 0, 4 + b, a) for a, b in zip(outer_pub, inner_pub)]
        for b in range(block_total):
            columns = []
            for k in range(tile_total):
                n = 2 + b * tile_total + k
                slot = ints[int_slot, n : n + 1, :]
                column = jnp.where(slot < 2, 2 + slot, after[1])
                column = jnp.where(slot == 2, before[0], column)
                column = jnp.where(slot == 3, before[1], column)
                column = jnp.where(slot == 4, after[0], column)
                columns.append(column)
            pieces = [tile_buf[tile_slot, b, k].astype(jnp.float32) for k in range(tile_total)]
            for j in range(6):
                total = jnp.zeros((side, side), jnp.float32)
                for k in range(tile_total):
                    total += pieces[k] * (columns[k] == j).astype(jnp.float32)
                op[b * side : (b + 1) * side, j * side : (j + 1) * side] = total.astype(jnp.bfloat16)

    def gather(op, layer, base, total):
        total[...] = jnp.dot(
            op[:, rows:], table[layer, (base + 1) * rows : (base + 3) * rows, :], preferred_element_type=jnp.float32
        )

    def propagate(op, layer, base, total, dst, done, pieces=2):
        piece = rows // pieces
        beta = jnp.float32(0.0)
        for i in range(layers):
            beta = jnp.where(layer == i, jnp.float32(math.log(THETA / (i + 1) + 1.0)), beta)
        for m in range(pieces):
            part = slice(m * piece, (m + 1) * piece)
            aggregate = total[part, :] + jnp.dot(
                op[part, :rows], table[layer, base * rows : (base + 1) * rows, :], preferred_element_type=jnp.float32
            )
            start = (base + 1) * rows + m * piece
            initial = table[0, start : start + piece, :].astype(jnp.float32)
            mixed = ((1.0 - SHARE) * aggregate + SHARE * initial).astype(jnp.bfloat16)
            support[part, :] = mixed
            product = jnp.dot(support[part, :], slab[layer], preferred_element_type=jnp.float32)
            state = (1.0 - beta) * support[part, :].astype(jnp.float32) + beta * product
            dst[part, :] = jnp.maximum(state, 0.0).astype(jnp.bfloat16)
            done(m)

    def slab_ready(layer):
        slab_forward_half = slab.at[layer, pl.ds(core * half, half)]
        pltpu.make_async_copy(slab_forward_half, slab_forward_half, slab_land.at[layer]).wait()

        @pl.when(layer // per_section != section)
        def _():
            slab_forward(layer).start()

        @pl.when((layer == 4) & (section == 0))
        def _():
            slab_copy(4, 4, 3).start()

    def slab_swapped(layer):
        part = slab.at[layer, pl.ds((1 - core) * half, half)]
        pltpu.make_async_copy(part, part, slab_swap.at[layer]).wait()

    def project(first, last_slot):
        part = slice(first * rows, last_slot * rows)
        table[0, part, :] = jnp.maximum(
            jnp.dot(rows_in[part, :], proj[...], preferred_element_type=jnp.float32), 0.0
        ).astype(jnp.bfloat16)

    @pl.when(chain)
    def _():
        @pl.when(jnp.logical_not(inner))
        def _():
            for layer in range(1, layers):
                table[layer, at(1)] = jnp.zeros((rows, table.shape[2]), jnp.bfloat16)
            rows_in[0 : 2 * rows, :] = jnp.zeros((2 * rows, rows_in.shape[1]), jnp.bfloat16)
            ints[0:2] = jnp.zeros((2, 16, 128), jnp.int32)

        tile_load.wait()
        for n in (1, 2, 0):
            each(takes, n, lambda: int_copy(n).wait_recv())
        build(near_op, 1, 2, 1, 3)
        feature_load.wait()
        proj_load.wait()
        for n in (2, 1):
            each(takes, n, lambda: feature_copy(n).wait_recv())
        project(1, 4)
        gather(near_op, 0, 1, near_sum)
        slab_ready(0)

        def step(layer, carry):
            slab_swapped(layer)

            def send(m):
                @pl.when((layer < layers - 2) & to_target)
                def _():
                    far_copy(layer + 1, m).start()

                near_copy(layer + 1, m).start()

                @pl.when(lax.rem(layer + 1, per_section) == 0)
                def _():
                    plane = (layer + 1) // per_section - 1
                    state = table.at[layer + 1, pl.ds(2 * rows + m * piece, piece)]

                    @pl.when(plane == section)
                    def _():
                        out_local(state, m).start()

                    @pl.when(plane != section)
                    def _():
                        out_copy(state, plane, m).start()

            propagate(near_op, layer, 1, near_sum, table.at[layer + 1, at(2)], send)

            slab_ready(layer + 1)

            @pl.when((layer == 0) & inner)
            def _():
                feature_copy(0).wait_recv()
                project(0, 1)
                tile_copy.wait_recv()
                build(ghost_op, 0, 1, 0, 2)

            @pl.when(inner)
            def _():
                gather(ghost_op, layer, 0, ghost_sum)

            near_copy(layer + 1).wait_recv()
            gather(near_op, layer + 1, 1, near_sum)

            @pl.when((layer > 0) & inner)
            def _():
                far_copy(layer).wait_recv()

            @pl.when(inner)
            def _():
                propagate(ghost_op, layer, 0, ghost_sum, table.at[layer + 1, at(1)], lambda m: None, 1)

            return carry

        lax.fori_loop(0, layers - 1, step, 0)
        end = layers - 1
        slab_swapped(end)

        def finish(m):
            state = last.at[pl.ds(m * piece, piece)]

            @pl.when(section == final_section)
            def _():
                out_local(state, m).start()

            @pl.when(section != final_section)
            def _():
                out_copy(state, final_section, m).start()

        propagate(near_op, end, 1, near_sum, last, finish)

        for n in range(3):
            each(gives, n, lambda: int_copy(n).wait_send())
            each(gives, n, lambda: feature_copy(n).wait_send())
        each(gives, 1, lambda: tile_copy.wait_send())
        for layer in range(1, layers):
            near_copy(layer).wait_send()
            if layer < layers - 1:
                @pl.when(to_target)
                def _():
                    far_copy(layer).wait_send()
        for layer in range(layers):
            @pl.when(layer // per_section != section)
            def _():
                slab_forward(layer).wait_send()
        for plane in range(sections):
            @pl.when(plane != section)
            def _():
                out_copy(last, plane).wait_send()
        out_local(last).wait()
        for plane in (0, 3):
            @pl.when(section == plane)
            def _():
                for copy in slab_sends(plane):
                    copy.wait_send()

        @pl.when(section == 0)
        def _():
            slab_copy(4, 4, 3).wait_send()

        arriving = out.at[0, other_group]
        pltpu.make_async_copy(arriving, arriving, out_land.at[other_group]).wait()

    def slab_arrived(layer):
        part = slab.at[layer, pl.ds(core * half, half)]
        pltpu.make_async_copy(part, part, slab_land.at[layer]).wait()

    for plane in (1, 2):
        @pl.when(section == plane)
        def _():
            copies = slab_sends(plane)
            for (layer, to), copy in zip(routes[plane], copies):
                if layer // per_section != plane:
                    slab_arrived(layer)
                copy.start()
            for copy in copies:
                copy.wait_send()
            for g in range(2):
                pltpu.make_async_copy(out.at[0, g], out.at[0, g], out_land.at[g]).wait()


def shards(features, input_weight, layer_weights, tiles, pub_ids, tile_src):
    groups, rows, width_in = features.shape
    width = input_weight.shape[1]
    block_total, tile_total, side = tiles.shape[1:4]
    per_section = layer_weights.shape[0]
    sections = lax.axis_size("section")
    partitions = lax.axis_size("dom")
    layers = sections * per_section
    anywhere = pl.BlockSpec(memory_space=pl.ANY)
    dma = pltpu.SemaphoreType.DMA
    bf16 = jnp.bfloat16
    held = [
        pltpu.with_memory_space_constraint(value, pltpu.HBM)
        for value in (features, input_weight, layer_weights, tiles, pub_ids, tile_src)
    ]
    return pl.pallas_call(
        functools.partial(kernel, sections, partitions),
        out_shape=jax.ShapeDtypeStruct((1, groups, rows, width), bf16),
        in_specs=[anywhere] * 6,
        out_specs=anywhere,
        scratch_shapes=[
            pltpu.SMEM(pub_ids.shape, jnp.int32),
            pltpu.SMEM(tile_src.shape, jnp.int32),
            pltpu.VMEM((layers, 4 * rows, width), bf16),
            pltpu.VMEM((rows, width), bf16),
            pltpu.VMEM((layers, width, width), bf16),
            pltpu.VMEM((4 * rows, width_in), bf16),
            pltpu.VMEM((width_in, width), bf16),
            pltpu.VMEM((2, block_total, tile_total, side, side), bf16),
            pltpu.VMEM((rows, 3 * rows), bf16),
            pltpu.VMEM((rows, 3 * rows), bf16),
            pltpu.VMEM((4, 16, 128), jnp.int32),
            pltpu.VMEM((rows, width), bf16),
            pltpu.VMEM((rows, width), jnp.float32),
            pltpu.VMEM((rows, width), jnp.float32),
            dma((6,)),
            dma((7,)),
            dma((4,)),
            dma((4,)),
            dma((1,)),
            dma((layers,)),
            dma((layers,)),
            dma((layers,)),
            dma((layers,)),
            dma((5,)),
            dma((layers,)),
            dma((layers,)),
            dma((layers,)),
            dma((sections,)),
            dma((groups,)),
        ],
        compiler_params=pltpu.CompilerParams(collective_id=0, has_side_effects=True, vmem_limit_bytes=40 * 2**20),
    )(*held)


def solution(mesh):
    in_specs = (
        P(None, "dom", None),
        P(),
        P("section", None, None),
        P(None, "dom", None, None, None),
        P(None, "dom"),
        P(None, "dom", None),
    )
    out_specs = P("section", None, "dom", None)
    return jax.shard_map(shards, mesh=mesh, in_specs=in_specs, out_specs=out_specs, check_vma=False)
```
